256 devices in a mesh: role: 2 (over x_lo), grp: 64 (over z, y, core), tp: 2 (over x_hi).
Axes of the slice: x: 4 (x_hi: 2, x_lo: 2; x = x_hi * 2 + x_lo), y: 4, z: 8, core: 2. Of those that a mesh axis runs over, the one named last changes fastest.
Arguments:
- q_new: bfloat16 [2048, 4096], P('grp', ('role', 'tp')), may hold values from -9 to 9
- k_new: bfloat16 [2048, 512], P('grp', ('role', 'tp')), may hold values from -6 to 6
- v_new: bfloat16 [2048, 512], P('grp', ('role', 'tp')), may hold values from -6 to 6
- k_cache: bfloat16 [2048, 128, 512], P('grp', None, ('role', 'tp')), may hold values from -9 to 9
- v_cache: bfloat16 [2048, 128, 512], P('grp', None, ('role', 'tp')), may hold values from -6 to 6
- cache_len: int32 [2048], P('grp'), may hold values from 1 to 127
- cycle_start: int32 [2048], P('grp'), may hold values from 0 to 127
- residual: bfloat16 [2048, 2880], P('grp', ('role', 'tp')), may hold values from -6 to 6
- out_proj: bfloat16 [4096, 2880], P(('role', 'tp')), may hold values from -0.09375 to 0.09375
- norm_gain: float32 [2880], replicated, may hold values from 0.25 to 1.75
- router: bfloat16 [2880, 64], P(('role', 'tp')), may hold values from -0.21875 to 0.21875
- route_ids: int32 [2048, 4], P('grp'), may hold values from 0 to 63, all different within a row; in each aligned block of 32 rows (0 to 31, 32 to 63, ...) at most 4 rows name the same one
- w_gate: bfloat16 [64, 2880, 1440], P('grp', None, ('role', 'tp')), may hold values from -0.109375 to 0.109375
- w_up: bfloat16 [64, 2880, 1440], P('grp', None, ('role', 'tp')), may hold values from -0.109375 to 0.109375
- w_down: bfloat16 [64, 1440, 2880], P('grp', ('role', 'tp')), may hold values from -0.15625 to 0.15625
Outputs:
- attended: bfloat16 [2048, 2880], P('grp', ('role', 'tp'))
- expert_mix: bfloat16 [2048, 2880], P('grp', ('role', 'tp'))
The draws below stay inside these ranges and needn't reach their ends.
Inputs may be any that keep to these rules, and one draw needn't show every extreme that they name: `route_ids`: the 4 experts of a token differ. Among the tokens of one grp index (aligned blocks of 32 tokens) no expert is named more than 4 times, a bound that some block reaches.
All inputs are finite; a program needn't handle non-finite values.
Results may differ from the reference program's by a relative error of at most 0.017.
Values may be sent and summed in bfloat16 or wider, within the bound.
A program may use at most 64 MiB of HBM per device.

```python
import math
import jax
import jax.numpy as jnp
import numpy as np
from jax import lax

D = 2880
FF = 1440
HEADS = 64
KV_HEADS = 8
HD = 64
WINDOW = 128
TOPK = 4
TOK_DEV = 32
TOKENS = 2048
EXPERTS = 64
CAP = 4
N_ROLE = 2
N_GRP = 64
N_TP = 2


def draw_q_new(key, part):
    return jnp.clip(jax.random.normal(jax.random.fold_in(key, 11), (TOKENS, HEADS * HD), jnp.float32), -6.0, 6.0).astype(jnp.bfloat16)


def draw_k_cache(key, part):
    return jnp.clip(jax.random.normal(jax.random.fold_in(key, 13), (TOKENS, WINDOW, KV_HEADS * HD), jnp.float32), -6.0, 6.0).astype(jnp.bfloat16)


def place_ends(values, key, least, high):
    shape = values.shape
    spot = [jax.random.randint(jax.random.fold_in(key, axis), (), 0, shape[axis]) for axis in range(len(shape))]
    values = values.at[tuple(spot)].set(least)
    longest = shape.index(max(shape))
    spot[longest] = (spot[longest] + 1) % shape[longest]
    return values.at[tuple(spot)].set(high)


def levels(stream_key, shape, split, low, top_value):
    level = 1.0
    for position, blocks in split:
        steps = jax.random.uniform(jax.random.fold_in(jax.random.fold_in(stream_key, 6), position), (blocks,), jnp.float32, low / len(split), top_value / len(split))
        level = level * jnp.repeat(jnp.exp(steps), shape[position] // blocks).reshape((-1,) + (1,) * (len(shape) - 1 - position))
    return level


def deal_out(rng, own, number, rows, count, top, reach, slope):
    order = jax.random.permutation(rng, count)
    packed, ordinary = portions_of(count, rows * top, reach, slope, True), portions_of(count, rows * top, reach, slope, False)
    places = jnp.arange(count)

    def named(tallies, rotation):
        used = int((tallies > 0).sum())
        fixed = max(1, used // 4)
        passed = fixed + (places - fixed + rotation * (used - fixed)) % max(1, count - fixed)
        return jnp.zeros((count,), jnp.int32).at[order[jnp.where(places < fixed, places, passed)]].set(jnp.asarray(tallies, jnp.int32))

    tallies = jnp.where(number % 4 == 0, named(packed, number // 4), named(ordinary, number - number // 4 - 1))
    mixed = jax.random.permutation(jax.random.fold_in(own, 3), count)
    source_of, receiver = mixed[0:count // 2 * 2:2], mixed[1:count // 2 * 2:2]
    slack = jnp.minimum(tallies[source_of] - 1, reach - tallies[receiver]) // 2
    slack = jnp.where((source_of == order[0]) | (receiver == order[0]) | (tallies[receiver] == 0), 0, jnp.maximum(slack, 0))
    passed = jax.random.randint(jax.random.fold_in(own, 4), (count // 2,), 0, 1 << 20) % (slack + 1)
    tallies = tallies.at[source_of].add(-passed).at[receiver].add(passed)
    items = jnp.searchsorted(jnp.cumsum(tallies), jnp.arange(rows * top), side="right").astype(jnp.int32)
    table = items.reshape(top, rows).T
    table = table[jax.random.permutation(jax.random.fold_in(own, 1), rows)]
    rotation = jax.random.randint(jax.random.fold_in(own, 2), (rows, 1), 0, top)
    return jnp.take_along_axis(table, (jnp.arange(top)[None, :] + rotation) % top, axis=1)


def portions_of(count, total, limit, lean, full):
    weights = [(1 << 20) // math.isqrt(rank ** lean) + 1 for rank in range(1, count + 1)]
    largest = limit if full else min(limit, max(-(-total // count), total * weights[0] // sum(weights)))
    least = 1 if total - largest >= count - 1 else 0
    given, rest = [largest] + [least] * (count - 1), total - largest - least * (count - 1)
    while rest > 0:
        free = [i for i in range(1, count) if given[i] < largest] or [i for i in range(1, count) if given[i] < limit]
        whole, budget = sum([weights[i] for i in free]), rest
        for i in free:
            more = min(limit - given[i], max(1, budget * weights[i] // whole), rest)
            given[i] = given[i] + more
            rest = rest - more
    return np.array(given)


def normal_values(stream_key, shape, width, bound, shards=(), kind=jnp.bfloat16):
    entries = width * jax.random.normal(stream_key, shape, jnp.float32)
    if shards:
        entries = entries * levels(stream_key, shape, shards, -0.22, 0.18)
    return jnp.clip(entries, -bound, bound).astype(kind)


def setup_inputs(seed: int = 0) -> dict:
    splits = jax.random.split(jax.random.key(seed), 16)
    q_new = draw_q_new(jax.random.fold_in(splits[15], 71), 0)
    k_new = normal_values(splits[1], (TOKENS, KV_HEADS * HD), 1.0, 6.0, ((0, 64), (1, 4)))
    v_new = normal_values(splits[2], (TOKENS, KV_HEADS * HD), 1.0, 6.0, ((0, 64), (1, 4)))
    k_cache = draw_k_cache(jax.random.fold_in(splits[15], 71), 0)
    v_cache = normal_values(splits[4], (TOKENS, WINDOW, KV_HEADS * HD), 1.0, 6.0, ((0, 64), (2, 4)))
    cache_len = place_ends(jax.random.randint(splits[5], (TOKENS,), 1, WINDOW), jax.random.fold_in(splits[5], 1), 1, WINDOW - 1).astype(jnp.int32)
    cycle_start = place_ends(jax.random.randint(splits[6], (TOKENS,), 0, WINDOW), jax.random.fold_in(splits[6], 1), 0, WINDOW - 1).astype(jnp.int32)
    residual = normal_values(splits[7], (TOKENS, D), 1.0, 6.0, ((0, 64), (1, 4)))
    out_proj = normal_values(splits[8], (HEADS * HD, D), (HEADS * HD) ** -0.5, 0.09375, ((0, 4),))
    norm_gain = jnp.clip(1.0 + 0.15 * jax.random.normal(splits[9], (D,), jnp.float32), 0.25, 1.75)
    router = normal_values(splits[10], (D, EXPERTS), (D // 4) ** -0.5, 0.21875, ((0, 4),))
    route_ids_keys = jax.random.split(jax.random.fold_in(splits[11], 1), TOKENS // TOK_DEV)
    route_ids_turns = jax.random.permutation(jax.random.fold_in(splits[11], 3), TOKENS // TOK_DEV)
    route_ids = jax.vmap(lambda own, number: deal_out(jax.random.fold_in(splits[11], 2), own, number, TOK_DEV, EXPERTS, TOPK, CAP, 2))(route_ids_keys, route_ids_turns).reshape((TOKENS, TOPK))
    w_gate = normal_values(splits[12], (EXPERTS, D, FF), D ** -0.5, 0.109375, ((0, 64), (2, 4)))
    w_up = normal_values(splits[13], (EXPERTS, D, FF), D ** -0.5, 0.109375, ((0, 64), (2, 4)))
    w_down = normal_values(splits[14], (EXPERTS, FF, D), FF ** -0.5, 0.15625, ((0, 64), (1, 4)))
    return dict(q_new=q_new, k_new=k_new, v_new=v_new, k_cache=k_cache, v_cache=v_cache, cache_len=cache_len, cycle_start=cycle_start, residual=residual, out_proj=out_proj, norm_gain=norm_gain, router=router, route_ids=route_ids, w_gate=w_gate, w_up=w_up, w_down=w_down)


epsilon = 1e-05

def attend(q_new, k_new, v_new, k_cache, v_cache, cache_len, cycle_start):
    tokens = q_new.shape[0]
    window = k_cache.shape[1]
    kv_local = k_new.shape[1] // HD
    grouped = HEADS // KV_HEADS
    queries = q_new.astype(jnp.float32).reshape(tokens, kv_local, grouped, HD)
    cached_keys = k_cache.astype(jnp.float32).reshape(tokens, window, kv_local, HD)
    cached_values = v_cache.astype(jnp.float32).reshape(tokens, window, kv_local, HD)
    own_key = k_new.astype(jnp.float32).reshape(tokens, kv_local, HD)
    own_value = v_new.astype(jnp.float32).reshape(tokens, kv_local, HD)
    factor = HD ** (-0.5)
    scores = jnp.einsum('tkgd,tskd->tkgs', queries, cached_keys) * factor
    own_score = jnp.einsum('tkgd,tkd->tkg', queries, own_key) * factor
    positions = jnp.arange(window, dtype=jnp.int32)
    usable = (positions[None, :] - cycle_start[:, None]) % window < cache_len[:, None]
    usable = usable[:, None, None, :]
    masked = jnp.where(usable, scores, -1e+30)
    highest = jnp.maximum(lax.optimization_barrier(jnp.max(masked, axis=3)), own_score)
    lifted = jnp.where(usable, jnp.exp(masked - highest[..., None]), 0.0)
    own_lift = jnp.exp(own_score - highest)
    denominator = lax.optimization_barrier(jnp.sum(lifted, axis=3)) + own_lift
    weights = lax.optimization_barrier((lifted / denominator[..., None]).astype(jnp.bfloat16)).astype(jnp.float32)
    own_weight = lax.optimization_barrier((own_lift / denominator).astype(jnp.bfloat16)).astype(jnp.float32)
    combined = jnp.einsum('tkgs,tskd->tkgd', weights, cached_values)
    combined = combined + own_weight[..., None] * own_value[:, :, None, :]
    return combined.reshape(tokens, -1).astype(jnp.bfloat16)

def block_ranks(route_ids):
    named = route_ids[:, :, None] == jnp.arange(EXPERTS, dtype=jnp.int32)
    counts = lax.optimization_barrier(jnp.sum(named.astype(jnp.int32), axis=1))
    blocked = counts.reshape(-1, TOK_DEV, EXPERTS)
    earlier = (jnp.cumsum(blocked, axis=1) - blocked).reshape(-1, EXPERTS)
    return lax.optimization_barrier(jnp.sum(jnp.where(named, earlier[:, None, :], 0), axis=2)).astype(jnp.int32)

def reference(q_new, k_new, v_new, k_cache, v_cache, cache_len, cycle_start, residual, out_proj, norm_gain, router, route_ids, w_gate, w_up, w_down):
    heads_out = attend(q_new, k_new, v_new, k_cache, v_cache, cache_len, cycle_start)
    stream = residual.astype(jnp.float32) + jnp.dot(heads_out, out_proj, preferred_element_type=jnp.float32)
    scale = lax.rsqrt(lax.optimization_barrier(jnp.mean(stream * stream, axis=1, keepdims=True)) + epsilon)
    normed = (stream * scale * norm_gain).astype(jnp.bfloat16)
    logits = jnp.dot(normed, router, preferred_element_type=jnp.float32)
    chosen = jnp.take_along_axis(logits, route_ids, axis=1)
    lifted = jnp.exp(chosen)
    route_weight = lifted / lax.optimization_barrier(jnp.sum(lifted, axis=1, keepdims=True))
    ranks = block_ranks(route_ids)
    shares = N_ROLE * N_TP
    share_width = FF // shares
    grouped_ids = route_ids.reshape(N_GRP, TOK_DEV, TOPK)
    grouped_ranks = ranks.reshape(N_GRP, TOK_DEV, TOPK)
    blocks = normed.astype(jnp.float32).reshape(N_GRP, TOK_DEV, D)
    capacity_range = jnp.arange(CAP, dtype=jnp.int32)

    def serve_expert(expert):
        picked = (grouped_ids == expert)[:, :, :, None] & (grouped_ranks[:, :, :, None] == capacity_range)
        select = lax.optimization_barrier(jnp.sum(picked.astype(jnp.float32), axis=2))
        inputs = jnp.einsum('gtc,gtd->gcd', select, blocks).reshape(N_GRP * CAP, D).astype(jnp.bfloat16)
        gate_lin = jnp.dot(inputs, w_gate[expert], preferred_element_type=jnp.float32)
        up_lin = jnp.dot(inputs, w_up[expert], preferred_element_type=jnp.float32)
        activated = (gate_lin * jax.nn.sigmoid(1.702 * gate_lin) * (up_lin + 1.0)).astype(jnp.bfloat16)
        pieces = jnp.einsum('nsf,sfd->snd', activated.astype(jnp.float32).reshape(-1, shares, share_width), w_down[expert].astype(jnp.float32).reshape(shares, share_width, D))
        rounded = lax.optimization_barrier(pieces.astype(jnp.bfloat16)).astype(jnp.float32)
        return lax.optimization_barrier(jnp.sum(rounded, axis=0))
    outputs = lax.map(serve_expert, jnp.arange(EXPERTS, dtype=jnp.int32))
    source = (jnp.arange(TOKENS, dtype=jnp.int32) // TOK_DEV)[:, None]
    gathered = outputs[route_ids, source * CAP + ranks]
    expert_mix = lax.optimization_barrier(jnp.sum(route_weight[:, :, None] * gathered, axis=1))
    return (stream.astype(jnp.bfloat16), expert_mix.astype(jnp.bfloat16))
```

```python
import jax
import jax.numpy as jnp
from jax import lax
from jax.experimental import pallas as pl
from jax.experimental.pallas import tpu as pltpu
from jax.sharding import PartitionSpec as P

HEADS = 64
KV_HEADS = 8
HD = 64
EPS = 1e-05
ND = 4
QW = 720
PW = 768
HW = PW // 2
NG = 64
NB = 4
BM = NG // NB
BR = BM * 4
MESH = pl.DeviceIdType.MESH
BF = jnp.bfloat16
F32 = jnp.float32


def attend(q_new, k_new, v_new, k_cache, v_cache, cache_len, cycle_start):
    tokens = q_new.shape[0]
    window = k_cache.shape[1]
    kv_local = k_new.shape[1] // HD
    grouped = HEADS // KV_HEADS
    queries = q_new.reshape(tokens, kv_local, grouped, HD)
    cached_keys = k_cache.reshape(tokens, window, kv_local, HD)
    cached_values = v_cache.reshape(tokens, window, kv_local, HD)
    own_key = k_new.reshape(tokens, kv_local, HD)
    own_value = v_new.reshape(tokens, kv_local, HD)
    factor = HD ** (-0.5)
    scores = (
        jnp.einsum("tkgd,tskd->tkgs", queries, cached_keys, preferred_element_type=jnp.float32)
        * factor
    )
    own_score = (
        jnp.einsum("tkgd,tkd->tkg", queries, own_key, preferred_element_type=jnp.float32) * factor
    )
    positions = jnp.arange(window, dtype=jnp.int32)
    usable = (positions[None, :] - cycle_start[:, None]) % window < cache_len[:, None]
    usable = usable[:, None, None, :]
    masked = jnp.where(usable, scores, -1e30)
    highest = jnp.maximum(jnp.max(masked, axis=3), own_score)
    lifted = jnp.where(usable, jnp.exp(masked - highest[..., None]), 0.0)
    own_lift = jnp.exp(own_score - highest)
    denominator = jnp.sum(lifted, axis=3) + own_lift
    weights = (lifted / denominator[..., None]).astype(jnp.bfloat16)
    own_weight = (own_lift / denominator).astype(jnp.bfloat16)
    combined = jnp.einsum(
        "tkgs,tskd->tkgd", weights, cached_values, preferred_element_type=jnp.float32
    )
    combined = (
        combined
        + own_weight.astype(jnp.float32)[..., None] * own_value.astype(jnp.float32)[:, :, None, :]
    )
    return combined.reshape(tokens, -1).astype(jnp.bfloat16)


def x_of(pos):
    role = pos % 2
    tp = pos // 2
    return {"role": role, "tp": tp}, role * 2 + tp


def grp_shift(z, y, c, k, sign):
    j = k // 8
    half = (j + 1) // 2
    dz = (j % 2) * half + (1 - j % 2) * (8 - half)
    dy = (k // 2) % 4
    dc = k % 2
    if sign < 0:
        dz = 8 - dz
        dy = 4 - dy
    return (((z + dz) % 8) * 4 + (y + dy) % 4) * 2 + (c + dc) % 2


def wait_bytes(ref, sem):
    pltpu.make_async_copy(ref, ref, sem).wait()


def stage(
    proj, resid, gain, router, ids_row, ids_col, wg_hbm, wu_hbm, wd_hbm,
    att_out, mix_out,
    wg, wu, wd, wda, rs, stats, stats_in, send, recv, s1s, s1r, s2s, s2r, own, rsend, rrecv,
    w_sem, rs_ss, rs_rs, st_ss, st_rs, a_ss, a_rs, x_ss, x_rs, f_ss, f_rs,
    p_ss, p_rs, q_ss, q_rs, b_ss, b_rs, l_sem,
):
    r = lax.axis_index("role")
    g = lax.axis_index("grp")
    t = lax.axis_index("tp")
    x = t * 2 + r
    z = g // 8
    y = (g // 2) % 4
    c = g % 2
    me_q = r * 2 + t
    right, right_q = x_of((x + 1) % 4)
    left, left_q = x_of((x + 3) % 4)
    opp, opp_q = x_of((x + 2) % 4)
    peers = (left, right, opp)
    blocks = (me_q, left_q, right_q, opp_q)

    barrier = pltpu.get_barrier_semaphore()
    for peer in peers:
        pl.semaphore_signal(barrier, inc=1, device_id=peer, device_id_type=MESH)

    def greet(k, carry):
        pl.semaphore_signal(
            barrier, inc=1, device_id={"grp": grp_shift(z, y, c, k, 1)}, device_id_type=MESH
        )
        return carry

    lax.fori_loop(1, NG, greet, 0)
    loads = [
        pltpu.make_async_copy(wg_hbm, wg.at[0 : ND * QW], w_sem.at[0]),
        pltpu.make_async_copy(wu_hbm, wu.at[0 : ND * QW], w_sem.at[1]),
        pltpu.make_async_copy(wd_hbm, wd, w_sem.at[2]),
    ]
    for load in loads:
        load.start()
    wg[ND * QW :, :] = jnp.zeros((48, wg.shape[1]), BF)
    wu[ND * QW :, :] = jnp.zeros((48, wu.shape[1]), BF)

    def experts_of(rows):
        return grp_shift(z, y, c, rows // 8, 1), (rows // 4) % 2, rows % 4

    slot = lax.broadcasted_iota(jnp.int32, (NG * 8, 1), 0)
    expert, part, rank = experts_of(slot)
    hit = jnp.zeros((NG * 8, 64), jnp.bool_)
    for k in range(4):
        hit = hit | (ids_row[k : k + 1, :] == expert)
    lane = lax.broadcasted_iota(jnp.int32, (64, 64), 1)
    sub = lax.broadcasted_iota(jnp.int32, (64, 64), 0)
    upper = jnp.where((sub < lane) & (sub // 32 == lane // 32), 1.0, 0.0).astype(BF)
    lower = jnp.where((lane < sub) & (sub // 32 == lane // 32), 1.0, 0.0).astype(BF)
    hit_f = jnp.where(hit, 1.0, 0.0)
    earlier = jnp.dot(hit_f.astype(BF), upper, preferred_element_type=F32)
    side = lax.broadcasted_iota(jnp.int32, (NG * 8, 64), 1) // 32
    pick = jnp.where(
        (earlier == rank.astype(F32)) & (side == part), hit_f, 0.0
    ).astype(BF)

    slot_l = lax.broadcasted_iota(jnp.int32, (1, NG * 8), 1)
    expert_l, part_l, rank_l = experts_of(slot_l)
    hit_l = jnp.zeros((64, NG * 8), jnp.bool_)
    for k in range(4):
        hit_l = hit_l | (ids_col[:, k : k + 1] == expert_l)
    hit_lf = jnp.where(hit_l, 1.0, 0.0)
    earlier_l = jnp.dot(lower, hit_lf.astype(BF), preferred_element_type=F32)
    side_l = lax.broadcasted_iota(jnp.int32, (64, NG * 8), 0) // 32
    pick_l = jnp.where(
        (earlier_l == rank_l.astype(F32)) & (side_l == part_l), hit_lf, 0.0
    )
    to_slot = jnp.where(
        lax.broadcasted_iota(jnp.int32, (64, NG * 8), 0) == expert_l, 1.0, 0.0
    ).astype(BF)

    pl.semaphore_wait(barrier, NG - 1 + 3)

    sums = []
    for i, (peer, block) in enumerate(zip(peers, (left_q, right_q, opp_q))):
        sums.append(
            pltpu.make_async_remote_copy(
                src_ref=proj.at[block], dst_ref=rs.at[i], send_sem=rs_ss.at[i],
                recv_sem=rs_rs.at[i], device_id=peer, device_id_type=MESH,
            )
        )
    for copy in sums:
        copy.start()
    attended = resid[...].astype(F32) + proj[me_q].astype(F32)
    for i, copy in enumerate(sums):
        copy.wait_recv()
        attended = attended + rs[i].astype(F32)
    att = attended.astype(BF)
    halves = jnp.concatenate([att[:, :HW], att[:, HW:]], axis=0)
    send[...] = (
        jnp.dot(pick, halves, preferred_element_type=F32).reshape(NG, 8, HW).astype(BF)
    )
    att_out[...] = att[:, :QW]
    weighted = (attended * gain[pl.ds(me_q, 1), :]).astype(BF)
    stats[...] = jnp.zeros(stats.shape, F32)
    stats[:, 0:64] = jnp.dot(weighted[:, :QW], router[...], preferred_element_type=F32)
    stats[:, 64:65] = jnp.sum(attended * attended, axis=1, keepdims=True)

    own_msg = pltpu.make_async_copy(send.at[0], recv.at[0, 0], a_rs.at[0])
    own_msg.start()

    def post(k, carry):
        pltpu.make_async_remote_copy(
            src_ref=send.at[k], dst_ref=recv.at[0, k], send_sem=a_ss, recv_sem=a_rs.at[k // BM],
            device_id={"grp": grp_shift(z, y, c, k, 1)}, device_id_type=MESH,
        ).start()
        return carry

    lax.fori_loop(1, NG, post, 0)
    shared = [
        pltpu.make_async_remote_copy(
            src_ref=stats, dst_ref=stats_in.at[i], send_sem=st_ss.at[i],
            recv_sem=st_rs.at[i], device_id=peer, device_id_type=MESH,
        )
        for i, peer in enumerate(peers)
    ]
    for copy in shared:
        copy.start()

    loads[2].wait()
    tail = jnp.zeros((4, 360, PW - QW), BF)
    wda[:, :, QW:] = tail

    def shift_rows(i, carry):
        rows = pl.ds(pl.multiple_of(i * 16, 16), 16)
        block = wd[rows, :].astype(F32)
        for q in range(4):
            wda[q, rows, 0:QW] = block[:, QW * q : QW * (q + 1)].astype(BF)
        return carry

    lax.fori_loop(0, 22, shift_rows, 0)
    block = wd[352:360, :].astype(F32)
    for q in range(4):
        wda[q, 352:360, 0:QW] = block[:, QW * q : QW * (q + 1)].astype(BF)
    loads[0].wait()
    loads[1].wait()

    total = stats[...]
    for i, copy in enumerate(shared):
        copy.wait_recv()
        total = total + stats_in[i]
    scale = lax.rsqrt(total[:, 64:65] / (ND * QW) + EPS)
    logits = total[:, 0:64] * scale
    named = jnp.zeros((32, 64), jnp.bool_)
    experts = lax.broadcasted_iota(jnp.int32, (32, 64), 1)
    for k in range(4):
        named = named | (ids_col[0:32, k : k + 1] == experts)
    lifted = jnp.where(named, jnp.exp(jnp.where(named, logits, 0.0)), 0.0)
    weight = lifted / jnp.sum(lifted, axis=1, keepdims=True)
    weight = jnp.concatenate([weight, weight], axis=0)
    w_high = weight.astype(BF)
    w_low = (weight - w_high.astype(F32)).astype(BF)
    mix_high = (jnp.dot(w_high, to_slot, preferred_element_type=F32) * pick_l).astype(BF)
    mix_low = (jnp.dot(w_low, to_slot, preferred_element_type=F32) * pick_l).astype(BF)

    first4 = lax.broadcasted_iota(jnp.int32, (BM // 2, 8, HW), 1) < 4

    def to_side(src, dst, ss, rs_, peer):
        return pltpu.make_async_remote_copy(
            src_ref=src, dst_ref=dst, send_sem=ss, recv_sem=rs_, device_id=peer,
            device_id_type=MESH,
        )

    def span(b):
        return pl.ds(b * BM, BM)

    def ring_out(b):
        wait_bytes(recv.at[0, span(b)], a_rs.at[b])
        copies = (
            to_side(recv.at[0, span(b)], recv.at[1, span(b)], x_ss.at[b, 0], x_rs.at[b, 0], right),
            to_side(recv.at[0, span(b)], recv.at[2, span(b)], x_ss.at[b, 1], x_rs.at[b, 1], left),
        )
        for copy in copies:
            copy.start()
        return copies

    def ring_on(b, copies):
        first, second = pl.ds(b * BM, BM // 2), pl.ds(b * BM + BM // 2, BM // 2)
        copies[0].wait_recv()
        on_right = to_side(
            recv.at[1, first], recv.at[3, first], f_ss.at[b, 0], f_rs.at[b, 0], right
        )
        on_right.start()
        copies[1].wait_recv()
        on_left = to_side(
            recv.at[2, second], recv.at[3, second], f_ss.at[b, 1], f_rs.at[b, 1], left
        )
        on_left.start()
        return on_right, on_left

    def expert_out(b, forwards):
        for copy in forwards:
            copy.wait_recv()
        gate = jnp.zeros((BR, wg.shape[1]), F32)
        up = jnp.zeros((BR, wu.shape[1]), F32)
        square = jnp.zeros((BR, 1), F32)
        for i, q in enumerate(blocks):
            rows = recv[i, span(b)].astype(F32).reshape(BM // 2, 2, 8, HW)
            even, odd = rows[:, 0], rows[:, 1]
            low = jnp.where(first4, even, pltpu.roll(odd, 4, 1)).reshape(BR, HW)
            high = jnp.where(first4, pltpu.roll(even, 4, 1), odd).reshape(BR, HW)
            feats = jnp.concatenate([low, high], axis=1)
            square = square + jnp.sum(feats * feats, axis=1, keepdims=True)
            feats = (feats * gain[pl.ds(q, 1), :]).astype(BF)
            depth = pl.ds(pl.multiple_of(q * QW, 16), PW)
            gate = gate + jnp.dot(feats, wg[depth, :], preferred_element_type=F32)
            up = up + jnp.dot(feats, wu[depth, :], preferred_element_type=F32)
        rms = lax.rsqrt(square / (ND * QW) + EPS)
        gate = gate * rms
        up = up * rms
        act = (gate * jax.nn.sigmoid(1.702 * gate) * (up + 1.0)).astype(BF)
        out = jnp.dot(act, wda[opp_q], preferred_element_type=F32).astype(BF)
        s1s[b, 0] = out[: BR // 2]
        s1s[b, 1] = out[BR // 2 :]
        copies = (
            to_side(s1s.at[b, 0], s1r.at[b, 0], p_ss.at[b, 0], p_rs.at[b, 0], right),
            to_side(s1s.at[b, 1], s1r.at[b, 1], p_ss.at[b, 1], p_rs.at[b, 1], left),
        )
        for copy in copies:
            copy.start()
        for i, q in enumerate((me_q, right_q, left_q)):
            out = jnp.dot(act, wda[q], preferred_element_type=F32)
            own[b, i] = out.astype(BF).astype(F32)
        return copies

    def sum_on(b, firsts):
        firsts[0].wait_recv()
        to_right = own[b, 1]
        s2s[b, 0, 0 : BR // 2] = (to_right[: BR // 2] + s1r[b, 0].astype(F32)).astype(BF)
        s2s[b, 0, BR // 2 :] = to_right[BR // 2 :].astype(BF)
        firsts[1].wait_recv()
        to_left = own[b, 2]
        s2s[b, 1, 0 : BR // 2] = to_left[: BR // 2].astype(BF)
        s2s[b, 1, BR // 2 :] = (to_left[BR // 2 :] + s1r[b, 1].astype(F32)).astype(BF)
        copies = (
            to_side(s2s.at[b, 0], s2r.at[b, 0], q_ss.at[b, 0], q_rs.at[b, 0], right),
            to_side(s2s.at[b, 1], s2r.at[b, 1], q_ss.at[b, 1], q_rs.at[b, 1], left),
        )
        for copy in copies:
            copy.start()
        return copies

    def give_back(b, seconds):
        for copy in seconds:
            copy.wait_recv()
        rows = own[b, 0] + s2r[b, 0].astype(F32) + s2r[b, 1].astype(F32)
        low = rows[:, :HW].reshape(BM // 2, 8, HW)
        high = rows[:, HW:].reshape(BM // 2, 8, HW)
        even = jnp.where(first4, low, pltpu.roll(high, 4, 1))
        odd = jnp.where(first4, pltpu.roll(low, 4, 1), high)
        rsend[b * BM : (b + 1) * BM] = (
            jnp.stack([even, odd], axis=1).reshape(BM, 8, HW).astype(BF)
        )
        if b == 0:
            pltpu.make_async_copy(rsend.at[0], rrecv.at[0], b_rs.at[0]).start()

        def post_back(k, carry):
            pltpu.make_async_remote_copy(
                src_ref=rsend.at[k], dst_ref=rrecv.at[k], send_sem=b_ss, recv_sem=b_rs.at[b],
                device_id={"grp": grp_shift(z, y, c, k, -1)}, device_id_type=MESH,
            ).start()
            return carry

        lax.fori_loop(max(1, b * BM), (b + 1) * BM, post_back, 0)

    out_c = [None] * NB
    on_c = [None] * NB
    one_c = [None] * NB
    two_c = [None] * NB
    out_c[0] = ring_out(0)
    out_c[1] = ring_out(1)
    on_c[0] = ring_on(0, out_c[0])
    out_c[2] = ring_out(2)
    on_c[1] = ring_on(1, out_c[1])
    out_c[3] = ring_out(3)
    one_c[0] = expert_out(0, on_c[0])
    on_c[2] = ring_on(2, out_c[2])
    one_c[1] = expert_out(1, on_c[1])
    on_c[3] = ring_on(3, out_c[3])
    two_c[0] = sum_on(0, one_c[0])
    one_c[2] = expert_out(2, on_c[2])
    two_c[1] = sum_on(1, one_c[1])
    give_back(0, two_c[0])
    one_c[3] = expert_out(3, on_c[3])
    two_c[2] = sum_on(2, one_c[2])
    give_back(1, two_c[1])
    two_c[3] = sum_on(3, one_c[3])
    give_back(2, two_c[2])
    give_back(3, two_c[3])

    mixed = jnp.zeros((64, HW), F32)
    for b in range(NB):
        wait_bytes(rrecv.at[span(b)], b_rs.at[b])
        rows = rrecv[b * BM : (b + 1) * BM].reshape(BM * 8, HW)
        cols = slice(b * BM * 8, (b + 1) * BM * 8)
        mixed = mixed + jnp.dot(mix_high[:, cols], rows, preferred_element_type=F32)
        mixed = mixed + jnp.dot(mix_low[:, cols], rows, preferred_element_type=F32)
    mixed = mixed.astype(BF)
    mix_out[:, 0:HW] = mixed[0:32]
    mix_out[:, HW:QW] = mixed[32:64, 0 : QW - HW]

    for copy in sums + shared:
        copy.wait_send()
    wait_bytes(send.at[pl.ds(1, NG - 1)], a_ss)
    wait_bytes(rsend.at[pl.ds(1, NG - 1)], b_ss)
    for group in (out_c, on_c, one_c, two_c):
        for pair in group:
            for copy in pair:
                copy.wait_send()


def local(
    q_new, k_new, v_new, k_cache, v_cache, cache_len, cycle_start, residual, out_proj,
    norm_gain, router, route_ids, w_gate, w_up, w_down,
):
    heads_out = attend(q_new, k_new, v_new, k_cache, v_cache, cache_len, cycle_start)
    projected = jnp.dot(heads_out, out_proj, preferred_element_type=F32).astype(BF)
    spare = PW - QW
    proj = jnp.pad(
        jnp.moveaxis(projected.reshape(-1, ND, QW), 1, 0), ((0, 0), (0, 0), (0, spare))
    )
    resid = jnp.pad(residual, ((0, 0), (0, spare)))
    gain = jnp.pad(norm_gain.reshape(ND, QW), ((0, 0), (0, spare)))
    ids_col = jnp.concatenate([route_ids, route_ids], axis=0)
    ids_row = ids_col.T
    vmem = pl.BlockSpec(memory_space=pltpu.VMEM)
    hbm = pl.BlockSpec(memory_space=pl.ANY)
    dma = pltpu.SemaphoreType.DMA
    half_ff = w_gate.shape[2]
    return pl.pallas_call(
        stage,
        out_shape=(
            jax.ShapeDtypeStruct(residual.shape, BF),
            jax.ShapeDtypeStruct(residual.shape, BF),
        ),
        in_specs=[vmem] * 6 + [hbm] * 3,
        out_specs=(vmem, vmem),
        scratch_shapes=[
            pltpu.VMEM((ND * QW + 48, half_ff), BF),
            pltpu.VMEM((ND * QW + 48, half_ff), BF),
            pltpu.VMEM((half_ff, ND * QW), BF),
            pltpu.VMEM((ND, half_ff, PW), BF),
            pltpu.VMEM((3, 32, PW), BF),
            pltpu.VMEM((32, 128), F32),
            pltpu.VMEM((3, 32, 128), F32),
            pltpu.VMEM((NG, 8, HW), BF),
            pltpu.VMEM((ND, NG, 8, HW), BF),
            pltpu.VMEM((NB, 2, BR // 2, PW), BF),
            pltpu.VMEM((NB, 2, BR // 2, PW), BF),
            pltpu.VMEM((NB, 2, BR, PW), BF),
            pltpu.VMEM((NB, 2, BR, PW), BF),
            pltpu.VMEM((NB, 3, BR, PW), F32),
            pltpu.VMEM((NG, 8, HW), BF),
            pltpu.VMEM((NG, 8, HW), BF),
            dma((3,)),
            dma((3,)),
            dma((3,)),
            dma((3,)),
            dma((3,)),
            dma,
            dma((NB,)),
            dma((NB, 2)),
            dma((NB, 2)),
            dma((NB, 2)),
            dma((NB, 2)),
            dma((NB, 2)),
            dma((NB, 2)),
            dma((NB, 2)),
            dma((NB, 2)),
            dma,
            dma((NB,)),
            dma,
        ],
        compiler_params=pltpu.CompilerParams(collective_id=0, has_side_effects=True),
        name="experts",
    )(proj, resid, gain, router, ids_row, ids_col, w_gate[0], w_up[0], w_down[0])


def solution(mesh):
    placed = (
        P("grp", ("role", "tp")),
        P("grp", ("role", "tp")),
        P("grp", ("role", "tp")),
        P("grp", None, ("role", "tp")),
        P("grp", None, ("role", "tp")),
        P("grp"),
        P("grp"),
        P("grp", ("role", "tp")),
        P(("role", "tp"), None),
        P(),
        P(("role", "tp"), None),
        P("grp", None),
        P("grp", None, ("role", "tp")),
        P("grp", None, ("role", "tp")),
        P("grp", ("role", "tp"), None),
    )
    return jax.shard_map(
        local,
        mesh=mesh,
        in_specs=placed,
        out_specs=(P("grp", ("role", "tp")), P("grp", ("role", "tp"))),
        check_vma=False,
    )
```

```python
import jax
import jax.numpy as jnp
from jax import lax
from jax.experimental import pallas as pl
from jax.experimental.pallas import tpu as pltpu
from jax.sharding import PartitionSpec as P

HD = 64
EPS = 1e-05
ND = 4
QW = 720
PW = 768
HW = PW // 2
NG = 64
NB = 4
BM = NG // NB
BR = BM * 4
MESH = pl.DeviceIdType.MESH
BF = jnp.bfloat16
F32 = jnp.float32


def attend(q_ref, k_new, v_new, keys, values, lens, starts, qs, hs):
    tokens, window = keys.shape[0], keys.shape[1]
    sub = lax.broadcasted_iota(jnp.int32, (tokens, tokens), 0)
    lane = lax.broadcasted_iota(jnp.int32, (tokens, tokens), 1)

    def column(row):
        return jnp.sum(jnp.where(sub == lane, row.astype(F32), 0.0), axis=1, keepdims=True)

    slot = lax.broadcasted_iota(jnp.int32, (tokens, window), 1).astype(F32)
    age = slot - column(starts[...])
    age = jnp.where(age < 0.0, age + window, age)
    live_all = jnp.where(age < column(lens[...]), 1.0, 0.0)
    queries = q_ref[...].astype(F32) * HD ** (-0.5)
    for j in range(8):
        qs[:, j, :] = queries[:, 128 * j : 128 * (j + 1)]
    step = 8
    shape = (step, 8, 128)
    mine = (lax.broadcasted_iota(jnp.int32, shape, 1) < 4) == (
        lax.broadcasted_iota(jnp.int32, shape, 2) < HD
    )
    key_own = k_new[...].astype(F32)
    value_own = v_new[...].astype(F32)
    for start in range(0, tokens, step):
        rows = slice(start, start + step)
        pair = qs[rows]
        heads = jnp.concatenate(
            [jnp.where(mine, pair, 0.0), jnp.where(mine, pltpu.roll(pair, HD, 2), 0.0)], axis=1
        )
        own = jnp.sum(heads * key_own[rows][:, None, :], axis=2, keepdims=True)
        scores = lax.dot_general(
            heads.astype(BF), keys[rows], (((2,), (2,)), ((0,), (0,))),
            preferred_element_type=F32,
        )
        live = jnp.broadcast_to(live_all[rows][:, None, :], scores.shape) > 0.5
        scores = jnp.where(live, scores, -1e30)
        highest = jnp.maximum(jnp.max(scores, axis=2, keepdims=True), own)
        lifted = jnp.where(live, jnp.exp(scores - highest), 0.0)
        own_lift = jnp.exp(own - highest)
        total = jnp.sum(lifted, axis=2, keepdims=True) + own_lift
        weights = (lifted / total).astype(BF)
        own_weight = (own_lift / total).astype(BF).astype(F32)
        out = lax.dot_general(
            weights, values[rows], (((2,), (1,)), ((0,), (0,))), preferred_element_type=F32
        )
        out = out + own_weight * value_own[rows][:, None, :]
        hs[rows] = jnp.where(mine, out[:, 0:8], 0.0) + pltpu.roll(
            jnp.where(mine, out[:, 8:16], 0.0), HD, 2
        )
    return jnp.concatenate([hs[:, j, :] for j in range(8)], axis=1).astype(BF)


def x_of(pos):
    role = pos % 2
    tp = pos // 2
    return {"role": role, "tp": tp}, role * 2 + tp


def grp_shift(z, y, c, k, sign):
    j = k // 8
    half = (j + 1) // 2
    dz = (j % 2) * half + (1 - j % 2) * (8 - half)
    dy = (k // 2) % 4
    dc = k % 2
    if sign < 0:
        dz = 8 - dz
        dy = 4 - dy
    return (((z + dz) % 8) * 4 + (y + dy) % 4) * 2 + (c + dc) % 2


def wait_bytes(ref, sem):
    pltpu.make_async_copy(ref, ref, sem).wait()


def stage(
    q_ref, k_new, v_new, k_hbm, v_hbm, lens, starts, resid, wo_hbm, gain_row, router, ids,
    wg_hbm, wu_hbm, wd_hbm,
    att_out, mix_out,
    keys, values, qs, hs, wo, proj, gain,
    wg, wu, wd, wga, wua, wda, rs, stats, stats_in, send, recv, s1s, s1r, s2s, s2r, own, rsend,
    rrecv,
    w_sem, rs_ss, rs_rs, st_ss, st_rs, a_ss, a_rs, x_ss, x_rs, f_ss, f_rs,
    p_ss, p_rs, q_ss, q_rs, b_ss, b_rs,
):
    r = lax.axis_index("role")
    g = lax.axis_index("grp")
    t = lax.axis_index("tp")
    x = t * 2 + r
    z = g // 8
    y = (g // 2) % 4
    c = g % 2
    me_q = r * 2 + t
    right, right_q = x_of((x + 1) % 4)
    left, left_q = x_of((x + 3) % 4)
    opp, opp_q = x_of((x + 2) % 4)
    peers = (opp, left, right)
    blocks = (me_q, left_q, right_q, opp_q)

    barrier = pltpu.get_barrier_semaphore()
    for peer in peers:
        pl.semaphore_signal(barrier, inc=1, device_id=peer, device_id_type=MESH)

    def greet(k, carry):
        pl.semaphore_signal(
            barrier, inc=1, device_id={"grp": grp_shift(z, y, c, k, 1)}, device_id_type=MESH
        )
        return carry

    lax.fori_loop(1, NG, greet, 0)
    loads = [
        pltpu.make_async_copy(src, dst, w_sem.at[i])
        for i, (src, dst) in enumerate(
            (
                (k_hbm, keys), (v_hbm, values), (wo_hbm, wo), (wg_hbm, wg), (wu_hbm, wu),
                (wd_hbm, wd),
            )
        )
    ]
    for load in loads:
        load.start()
    gain[...] = jnp.zeros(gain.shape, F32)
    for q in range(4):
        gain[q : q + 1, 0:QW] = gain_row[:, QW * q : QW * (q + 1)]
        proj[q, :, QW:] = jnp.zeros((32, PW - QW), BF)

    def experts_of(rows):
        return grp_shift(z, y, c, rows // 8, 1), (rows // 4) % 2, rows % 4

    slot = lax.broadcasted_iota(jnp.int32, (NG * 8, 1), 0)
    expert, part, rank = experts_of(slot)
    lane = lax.broadcasted_iota(jnp.int32, (64, 32), 1)
    sub = lax.broadcasted_iota(jnp.int32, (64, 32), 0)
    ids_f = ids[...].astype(F32)
    ids_col = [
        jnp.sum(jnp.where(sub % 32 == lane, ids_f[k : k + 1, :], 0.0), axis=1, keepdims=True)
        for k in range(4)
    ]
    lane = lax.broadcasted_iota(jnp.int32, (32, 64), 1)
    sub = lax.broadcasted_iota(jnp.int32, (32, 64), 0)
    ids_row = [
        jnp.sum(jnp.where(lane % 32 == sub, ids_col[k][0:32], 0.0), axis=0, keepdims=True)
        for k in range(4)
    ]
    expert_f = expert.astype(F32)
    hit_f = jnp.zeros((NG * 8, 64), F32)
    for k in range(4):
        hit_f = jnp.where(ids_row[k] == expert_f, 1.0, hit_f)
    lane = lax.broadcasted_iota(jnp.int32, (64, 64), 1)
    sub = lax.broadcasted_iota(jnp.int32, (64, 64), 0)
    upper = jnp.where((sub < lane) & (sub // 32 == lane // 32), 1.0, 0.0).astype(BF)
    lower = jnp.where((lane < sub) & (sub // 32 == lane // 32), 1.0, 0.0).astype(BF)
    earlier = jnp.dot(hit_f.astype(BF), upper, preferred_element_type=F32)
    side = lax.broadcasted_iota(jnp.int32, (NG * 8, 64), 1) // 32
    pick = jnp.where(
        (earlier == rank.astype(F32)) & (side == part), hit_f, 0.0
    ).astype(BF)

    slot_l = lax.broadcasted_iota(jnp.int32, (1, NG * 8), 1)
    expert_l, part_l, rank_l = experts_of(slot_l)
    expert_lf = expert_l.astype(F32)
    hit_lf = jnp.zeros((64, NG * 8), F32)
    for k in range(4):
        hit_lf = jnp.where(ids_col[k] == expert_lf, 1.0, hit_lf)
    earlier_l = jnp.dot(lower, hit_lf.astype(BF), preferred_element_type=F32)
    side_l = lax.broadcasted_iota(jnp.int32, (64, NG * 8), 0) // 32
    pick_l = jnp.where(
        (earlier_l == rank_l.astype(F32)) & (side_l == part_l), hit_lf, 0.0
    )
    to_slot = jnp.where(
        lax.broadcasted_iota(jnp.int32, (64, NG * 8), 0) == expert_l, 1.0, 0.0
    ).astype(BF)

    loads[0].wait()
    loads[1].wait()
    heads_out = attend(q_ref, k_new, v_new, keys, values, lens, starts, qs, hs)
    loads[2].wait()
    pl.semaphore_wait(barrier, NG - 1 + 3)

    sums = []
    for i, block in enumerate((opp_q, left_q, right_q, me_q)):
        rows = pl.ds(pl.multiple_of(block * QW, 16), QW)
        part_sum = lax.dot_general(
            heads_out, wo[rows, :], (((1,), (1,)), ((), ())), preferred_element_type=F32
        )
        proj[i, :, 0:QW] = part_sum.astype(BF)
        if i < 3:
            copy = pltpu.make_async_remote_copy(
                src_ref=proj.at[i], dst_ref=rs.at[i], send_sem=rs_ss.at[i],
                recv_sem=rs_rs.at[i], device_id=peers[i], device_id_type=MESH,
            )
            copy.start()
            sums.append(copy)
    attended = proj[3, :, 0:QW].astype(F32) + resid[...].astype(F32)
    for i in (1, 2, 0):
        sums[i].wait_recv()
        attended = attended + rs[i, :, 0:QW].astype(F32)
    attended = jnp.concatenate([attended, jnp.zeros((32, PW - QW), F32)], axis=1)
    att = attended.astype(BF)
    halves = jnp.concatenate([att[:, :HW], att[:, HW:]], axis=0)
    send[...] = (
        jnp.dot(pick, halves, preferred_element_type=F32).reshape(NG, 8, HW).astype(BF)
    )
    att_out[...] = att[:, :QW]
    weighted = (attended * gain[pl.ds(me_q, 1), :]).astype(BF)
    stats[...] = jnp.zeros(stats.shape, F32)
    stats[:, 0:64] = lax.dot_general(
        weighted[:, :QW], router[...], (((1,), (1,)), ((), ())), preferred_element_type=F32
    )
    stats[:, 64:65] = jnp.sum(attended * attended, axis=1, keepdims=True)

    own_msg = pltpu.make_async_copy(send.at[0], recv.at[0, 0], a_rs.at[0])
    own_msg.start()

    def post(k, carry):
        pltpu.make_async_remote_copy(
            src_ref=send.at[k], dst_ref=recv.at[0, k], send_sem=a_ss, recv_sem=a_rs.at[k // BM],
            device_id={"grp": grp_shift(z, y, c, k, 1)}, device_id_type=MESH,
        ).start()
        return carry

    lax.fori_loop(1, NG, post, 0)
    shared = [
        pltpu.make_async_remote_copy(
            src_ref=stats, dst_ref=stats_in.at[i], send_sem=st_ss.at[i],
            recv_sem=st_rs.at[i], device_id=peer, device_id_type=MESH,
        )
        for i, peer in enumerate(peers)
    ]
    for copy in shared:
        copy.start()

    for raw, out, load in ((wg, wga, loads[3]), (wu, wua, loads[4]), (wd, wda, loads[5])):
        load.wait()
        out[:, :, QW:] = jnp.zeros((4, 360, PW - QW), BF)

        def shift_rows(i, carry, raw=raw, out=out):
            rows = pl.ds(pl.multiple_of(i * 16, 16), 16)
            for q in range(4):
                out[q, rows, 0:QW] = raw[rows, QW * q : QW * (q + 1)]
            return carry

        lax.fori_loop(0, 22, shift_rows, 0)
        for q in range(4):
            out[q, 352:360, 0:QW] = raw[352:360, QW * q : QW * (q + 1)]

    total = stats[...]
    for i, copy in enumerate(shared):
        copy.wait_recv()
        total = total + stats_in[i]
    scale = lax.rsqrt(total[:, 64:65] / (ND * QW) + EPS)
    logits = total[:, 0:64] * scale
    named = jnp.zeros((32, 64), jnp.bool_)
    experts = lax.broadcasted_iota(jnp.int32, (32, 64), 1).astype(F32)
    for k in range(4):
        named = named | (ids_col[k][0:32] == experts)
    lifted = jnp.where(named, jnp.exp(jnp.where(named, logits, 0.0)), 0.0)
    weight = lifted / jnp.sum(lifted, axis=1, keepdims=True)
    weight = jnp.concatenate([weight, weight], axis=0)
    w_high = weight.astype(BF)
    w_low = (weight - w_high.astype(F32)).astype(BF)
    mix_high = (jnp.dot(w_high, to_slot, preferred_element_type=F32) * pick_l).astype(BF)
    mix_low = (jnp.dot(w_low, to_slot, preferred_element_type=F32) * pick_l).astype(BF)

    first4 = lax.broadcasted_iota(jnp.int32, (BM // 2, 8, HW), 1) < 4

    def to_side(src, dst, ss, rs_, peer):
        return pltpu.make_async_remote_copy(
            src_ref=src, dst_ref=dst, send_sem=ss, recv_sem=rs_, device_id=peer,
            device_id_type=MESH,
        )

    def span(b):
        return pl.ds(b * BM, BM)

    def ring_out(b):
        wait_bytes(recv.at[0, span(b)], a_rs.at[b])
        copies = (
            to_side(recv.at[0, span(b)], recv.at[1, span(b)], x_ss.at[b, 0], x_rs.at[b, 0], right),
            to_side(recv.at[0, span(b)], recv.at[2, span(b)], x_ss.at[b, 1], x_rs.at[b, 1], left),
        )
        for copy in copies:
            copy.start()
        return copies

    def ring_on(b, copies):
        first, second = pl.ds(b * BM, BM // 2), pl.ds(b * BM + BM // 2, BM // 2)
        copies[0].wait_recv()
        on_right = to_side(
            recv.at[1, first], recv.at[3, first], f_ss.at[b, 0], f_rs.at[b, 0], right
        )
        on_right.start()
        copies[1].wait_recv()
        on_left = to_side(
            recv.at[2, second], recv.at[3, second], f_ss.at[b, 1], f_rs.at[b, 1], left
        )
        on_left.start()
        return on_right, on_left

    def expert_out(b, forwards):
        for copy in forwards:
            copy.wait_recv()
        gate = jnp.zeros((BR, 360), F32)
        up = jnp.zeros((BR, 360), F32)
        square = jnp.zeros((BR, 1), F32)
        for i, q in enumerate(blocks):
            rows = recv[i, span(b)].astype(F32).reshape(BM // 2, 2, 8, HW)
            even, odd = rows[:, 0], rows[:, 1]
            low = jnp.where(first4, even, pltpu.roll(odd, 4, 1)).reshape(BR, HW)
            high = jnp.where(first4, pltpu.roll(even, 4, 1), odd).reshape(BR, HW)
            feats = jnp.concatenate([low, high], axis=1)
            square = square + jnp.sum(feats * feats, axis=1, keepdims=True)
            feats = (feats * gain[pl.ds(q, 1), :]).astype(BF)
            last = (((1,), (1,)), ((), ()))
            gate = gate + lax.dot_general(feats, wga[q], last, preferred_element_type=F32)
            up = up + lax.dot_general(feats, wua[q], last, preferred_element_type=F32)
        rms = lax.rsqrt(square / (ND * QW) + EPS)
        gate = gate * rms
        up = up * rms
        act = (gate * jax.nn.sigmoid(1.702 * gate) * (up + 1.0)).astype(BF)
        out = jnp.dot(act, wda[opp_q], preferred_element_type=F32).astype(BF)
        s1s[b, 0] = out[: BR // 2]
        s1s[b, 1] = out[BR // 2 :]
        copies = (
            to_side(s1s.at[b, 0], s1r.at[b, 0], p_ss.at[b, 0], p_rs.at[b, 0], right),
            to_side(s1s.at[b, 1], s1r.at[b, 1], p_ss.at[b, 1], p_rs.at[b, 1], left),
        )
        for copy in copies:
            copy.start()
        for i, q in enumerate((me_q, right_q, left_q)):
            out = jnp.dot(act, wda[q], preferred_element_type=F32)
            own[b, i] = out.astype(BF).astype(F32)
        return copies

    def sum_on(b, firsts):
        firsts[0].wait_recv()
        to_right = own[b, 1]
        s2s[b, 0, 0 : BR // 2] = (to_right[: BR // 2] + s1r[b, 0].astype(F32)).astype(BF)
        s2s[b, 0, BR // 2 :] = to_right[BR // 2 :].astype(BF)
        firsts[1].wait_recv()
        to_left = own[b, 2]
        s2s[b, 1, 0 : BR // 2] = to_left[: BR // 2].astype(BF)
        s2s[b, 1, BR // 2 :] = (to_left[BR // 2 :] + s1r[b, 1].astype(F32)).astype(BF)
        copies = (
            to_side(s2s.at[b, 0], s2r.at[b, 0], q_ss.at[b, 0], q_rs.at[b, 0], right),
            to_side(s2s.at[b, 1], s2r.at[b, 1], q_ss.at[b, 1], q_rs.at[b, 1], left),
        )
        for copy in copies:
            copy.start()
        return copies

    def give_back(b, seconds):
        for copy in seconds:
            copy.wait_recv()
        rows = own[b, 0] + s2r[b, 0].astype(F32) + s2r[b, 1].astype(F32)
        low = rows[:, :HW].reshape(BM // 2, 8, HW)
        high = rows[:, HW:].reshape(BM // 2, 8, HW)
        even = jnp.where(first4, low, pltpu.roll(high, 4, 1))
        odd = jnp.where(first4, pltpu.roll(low, 4, 1), high)
        rsend[b * BM : (b + 1) * BM] = (
            jnp.stack([even, odd], axis=1).reshape(BM, 8, HW).astype(BF)
        )
        if b == 0:
            pltpu.make_async_copy(rsend.at[0], rrecv.at[0], b_rs.at[0]).start()

        def post_back(k, carry):
            pltpu.make_async_remote_copy(
                src_ref=rsend.at[k], dst_ref=rrecv.at[k], send_sem=b_ss, recv_sem=b_rs.at[b],
                device_id={"grp": grp_shift(z, y, c, k, -1)}, device_id_type=MESH,
            ).start()
            return carry

        lax.fori_loop(max(1, b * BM), (b + 1) * BM, post_back, 0)

    out_c = [None] * NB
    on_c = [None] * NB
    one_c = [None] * NB
    two_c = [None] * NB
    out_c[0] = ring_out(0)
    out_c[1] = ring_out(1)
    on_c[0] = ring_on(0, out_c[0])
    out_c[2] = ring_out(2)
    on_c[1] = ring_on(1, out_c[1])
    out_c[3] = ring_out(3)
    one_c[0] = expert_out(0, on_c[0])
    on_c[2] = ring_on(2, out_c[2])
    one_c[1] = expert_out(1, on_c[1])
    on_c[3] = ring_on(3, out_c[3])
    two_c[0] = sum_on(0, one_c[0])
    one_c[2] = expert_out(2, on_c[2])
    two_c[1] = sum_on(1, one_c[1])
    give_back(0, two_c[0])
    one_c[3] = expert_out(3, on_c[3])
    two_c[2] = sum_on(2, one_c[2])
    give_back(1, two_c[1])
    two_c[3] = sum_on(3, one_c[3])
    give_back(2, two_c[2])
    give_back(3, two_c[3])

    mixed = jnp.zeros((64, HW), F32)
    for b in range(NB):
        wait_bytes(rrecv.at[span(b)], b_rs.at[b])
        rows = rrecv[b * BM : (b + 1) * BM].reshape(BM * 8, HW)
        cols = slice(b * BM * 8, (b + 1) * BM * 8)
        mixed = mixed + jnp.dot(mix_high[:, cols], rows, preferred_element_type=F32)
        mixed = mixed + jnp.dot(mix_low[:, cols], rows, preferred_element_type=F32)
    mixed = mixed.astype(BF)
    mix_out[:, 0:HW] = mixed[0:32]
    mix_out[:, HW:QW] = mixed[32:64, 0 : QW - HW]

    for copy in sums + shared:
        copy.wait_send()
    wait_bytes(send.at[pl.ds(1, NG - 1)], a_ss)
    wait_bytes(rsend.at[pl.ds(1, NG - 1)], b_ss)
    for group in (out_c, on_c, one_c, two_c):
        for pair in group:
            for copy in pair:
                copy.wait_send()


def local(
    q_new, k_new, v_new, k_cache, v_cache, cache_len, cycle_start, residual, out_proj,
    norm_gain, router, route_ids, w_gate, w_up, w_down,
):
    vmem = pl.BlockSpec(memory_space=pltpu.VMEM)
    hbm = pl.BlockSpec(memory_space=pl.ANY)
    dma = pltpu.SemaphoreType.DMA
    ff = w_gate.shape[2]
    tokens, heads = q_new.shape
    wide = pltpu.VMEM((ff, ND * QW), BF)
    cut = pltpu.VMEM((ND, ff, PW), BF)
    return pl.pallas_call(
        stage,
        out_shape=(
            jax.ShapeDtypeStruct(residual.shape, BF),
            jax.ShapeDtypeStruct(residual.shape, BF),
        ),
        in_specs=[vmem] * 3 + [hbm] * 2 + [vmem] * 3 + [hbm] + [vmem] * 3 + [hbm] * 3,
        out_specs=(vmem, vmem),
        scratch_shapes=[
            pltpu.VMEM(k_cache.shape, BF),
            pltpu.VMEM(v_cache.shape, BF),
            pltpu.VMEM((tokens, heads // 128, 128), F32),
            pltpu.VMEM((tokens, heads // 128, 128), F32),
            pltpu.VMEM((ND * QW, heads), BF),
            pltpu.VMEM((ND, tokens, PW), BF),
            pltpu.VMEM((ND, PW), F32),
            wide,
            wide,
            wide,
            cut,
            cut,
            cut,
            pltpu.VMEM((3, 32, PW), BF),
            pltpu.VMEM((32, 128), F32),
            pltpu.VMEM((3, 32, 128), F32),
            pltpu.VMEM((NG, 8, HW), BF),
            pltpu.VMEM((ND, NG, 8, HW), BF),
            pltpu.VMEM((NB, 2, BR // 2, PW), BF),
            pltpu.VMEM((NB, 2, BR // 2, PW), BF),
            pltpu.VMEM((NB, 2, BR, PW), BF),
            pltpu.VMEM((NB, 2, BR, PW), BF),
            pltpu.VMEM((NB, 3, BR, PW), F32),
            pltpu.VMEM((NG, 8, HW), BF),
            pltpu.VMEM((NG, 8, HW), BF),
            dma((6,)),
            dma((3,)),
            dma((3,)),
            dma((3,)),
            dma((3,)),
            dma,
            dma((NB,)),
            dma((NB, 2)),
            dma((NB, 2)),
            dma((NB, 2)),
            dma((NB, 2)),
            dma((NB, 2)),
            dma((NB, 2)),
            dma((NB, 2)),
            dma((NB, 2)),
            dma,
            dma((NB,)),
        ],
        compiler_params=pltpu.CompilerParams(collective_id=0, has_side_effects=True),
        name="experts",
    )(
        q_new, k_new, v_new, k_cache, v_cache, cache_len[None], cycle_start[None], residual,
        out_proj.T, norm_gain[None], router.T, route_ids.T, w_gate[0].T, w_up[0].T, w_down[0],
    )


def solution(mesh):
    placed = (
        P("grp", ("role", "tp")),
        P("grp", ("role", "tp")),
        P("grp", ("role", "tp")),
        P("grp", None, ("role", "tp")),
        P("grp", None, ("role", "tp")),
        P("grp"),
        P("grp"),
        P("grp", ("role", "tp")),
        P(("role", "tp"), None),
        P(),
        P(("role", "tp"), None),
        P("grp", None),
        P("grp", None, ("role", "tp")),
        P("grp", None, ("role", "tp")),
        P("grp", ("role", "tp"), None),
    )
    return jax.shard_map(
        local,
        mesh=mesh,
        in_specs=placed,
        out_specs=(P("grp", ("role", "tp")), P("grp", ("role", "tp"))),
        check_vma=False,
    )
```

```python
import jax
import jax.numpy as jnp
from jax import lax
from jax.experimental import pallas as pl
from jax.experimental.pallas import tpu as pltpu
from jax.sharding import PartitionSpec as P

HD = 64
EPS = 1e-05
ND = 4
QW = 720
PW = 768
HW = PW // 2
NG = 64
NJ = 4
JM = NG // NJ
NB = 4
BM = NG // NB
BR = BM * 4
MESH = pl.DeviceIdType.MESH
BF = jnp.bfloat16
F32 = jnp.float32


def attend(q_ref, k_new, v_new, keys, values, lens, starts, qs, hs):
    tokens, window = keys.shape[0], keys.shape[1]
    sub = lax.broadcasted_iota(jnp.int32, (tokens, tokens), 0)
    lane = lax.broadcasted_iota(jnp.int32, (tokens, tokens), 1)

    def column(row):
        return jnp.sum(jnp.where(sub == lane, row.astype(F32), 0.0), axis=1, keepdims=True)

    slot = lax.broadcasted_iota(jnp.int32, (tokens, window), 1).astype(F32)
    age = slot - column(starts[...])
    age = jnp.where(age < 0.0, age + window, age)
    live_all = jnp.where(age < column(lens[...]), 1.0, 0.0)
    queries = q_ref[...].astype(F32) * HD ** (-0.5)
    for j in range(8):
        qs[:, j, :] = queries[:, 128 * j : 128 * (j + 1)]
    step = 8
    shape = (step, 8, 128)
    mine = (lax.broadcasted_iota(jnp.int32, shape, 1) < 4) == (
        lax.broadcasted_iota(jnp.int32, shape, 2) < HD
    )
    key_own = k_new[...].astype(F32)
    value_own = v_new[...].astype(F32)
    for start in range(0, tokens, step):
        rows = slice(start, start + step)
        pair = qs[rows]
        heads = jnp.concatenate(
            [jnp.where(mine, pair, 0.0), jnp.where(mine, pltpu.roll(pair, HD, 2), 0.0)], axis=1
        )
        own = jnp.sum(heads * key_own[rows][:, None, :], axis=2, keepdims=True)
        scores = lax.dot_general(
            heads.astype(BF), keys[rows], (((2,), (2,)), ((0,), (0,))),
            preferred_element_type=F32,
        )
        live = jnp.broadcast_to(live_all[rows][:, None, :], scores.shape) > 0.5
        scores = jnp.where(live, scores, -1e30)
        highest = jnp.maximum(jnp.max(scores, axis=2, keepdims=True), own)
        lifted = jnp.where(live, jnp.exp(scores - highest), 0.0)
        own_lift = jnp.exp(own - highest)
        total = jnp.sum(lifted, axis=2, keepdims=True) + own_lift
        weights = (lifted / total).astype(BF)
        own_weight = (own_lift / total).astype(BF).astype(F32)
        out = lax.dot_general(
            weights, values[rows], (((2,), (1,)), ((0,), (0,))), preferred_element_type=F32
        )
        out = out + own_weight * value_own[rows][:, None, :]
        hs[rows] = jnp.where(mine, out[:, 0:8], 0.0) + pltpu.roll(
            jnp.where(mine, out[:, 8:16], 0.0), HD, 2
        )
    return jnp.concatenate([hs[:, j, :] for j in range(8)], axis=1).astype(BF)


def x_of(pos):
    role = pos % 2
    tp = pos // 2
    return {"role": role, "tp": tp}, role * 2 + tp


def grp_shift(z, y, c, k, sign):
    j = lax.div(k, 8)
    half = lax.div(j + 1, 2)
    odd = lax.rem(j, 2)
    dz = odd * half + (1 - odd) * (8 - half)
    dy = lax.rem(lax.div(k, 2), 4)
    dc = lax.rem(k, 2)
    if sign < 0:
        dz = 8 - dz
        dy = 4 - dy
    return (lax.rem(z + dz, 8) * 4 + lax.rem(y + dy, 4)) * 2 + lax.rem(c + dc, 2)


def wait_bytes(ref, sem):
    pltpu.make_async_copy(ref, ref, sem).wait()


def stage(
    q_ref, k_new, v_new, k_hbm, v_hbm, lens, starts, resid, wo_hbm, gain_row, router, ids,
    wg_hbm, wu_hbm, wd_hbm,
    att_out, mix_out,
    keys, values, qs, hs, wo, proj, gain,
    wg, wu, wd, wga, wua, wda, rs, stats, stats_in, send, recv, s1s, s1r, s2s, s2r, own, rsend,
    rrecv,
    w_sem, rs_ss, rs_rs, st_ss, st_rs, a_ss, a_rs, x_ss, x_rs, f_ss, f_rs,
    p_ss, p_rs, q_ss, q_rs, b_ss, b_rs,
):
    r = lax.axis_index("role")
    g = lax.axis_index("grp")
    t = lax.axis_index("tp")
    x = t * 2 + r
    z = g // 8
    y = (g // 2) % 4
    c = g % 2
    me_q = r * 2 + t
    right, right_q = x_of((x + 1) % 4)
    left, left_q = x_of((x + 3) % 4)
    opp, opp_q = x_of((x + 2) % 4)
    peers = (opp, left, right)
    blocks = (me_q, left_q, right_q, opp_q)

    barrier = pltpu.get_barrier_semaphore()

    def greet(k, carry):
        pl.semaphore_signal(
            barrier, inc=1, device_id={"grp": grp_shift(z, y, c, NG - k, 1)},
            device_id_type=MESH,
        )
        return carry

    lax.fori_loop(1, NG, greet, 0)
    for peer in peers:
        pl.semaphore_signal(barrier, inc=1, device_id=peer, device_id_type=MESH)
    loads = [
        pltpu.make_async_copy(src, dst, w_sem.at[i])
        for i, (src, dst) in enumerate(
            (
                (k_hbm, keys), (v_hbm, values), (wo_hbm, wo), (wg_hbm, wg), (wu_hbm, wu),
                (wd_hbm, wd),
            )
        )
    ]
    for load in loads:
        load.start()
    gain[...] = jnp.zeros(gain.shape, F32)
    for q in range(4):
        gain[q : q + 1, 0:QW] = gain_row[QW * q : QW * (q + 1)].reshape(1, QW)
        proj[q, :, QW:] = jnp.zeros((32, PW - QW), BF)

    def experts_of(rows):
        return grp_shift(z, y, c, lax.div(rows, 8), 1), lax.rem(lax.div(rows, 4), 2), lax.rem(rows, 4)

    slot = lax.broadcasted_iota(jnp.int32, (NG * 8, 1), 0)
    expert, part, rank = experts_of(slot)
    lane = lax.broadcasted_iota(jnp.int32, (64, 32), 1)
    sub = lax.broadcasted_iota(jnp.int32, (64, 32), 0)
    ids_f = ids[...].astype(F32)
    ids_col = [
        jnp.sum(jnp.where(sub % 32 == lane, ids_f[k : k + 1, :], 0.0), axis=1, keepdims=True)
        for k in range(4)
    ]
    lane = lax.broadcasted_iota(jnp.int32, (32, 64), 1)
    sub = lax.broadcasted_iota(jnp.int32, (32, 64), 0)
    ids_row = [
        jnp.sum(jnp.where(lane % 32 == sub, ids_col[k][0:32], 0.0), axis=0, keepdims=True)
        for k in range(4)
    ]
    expert_f = expert.astype(F32)
    hit_f = jnp.zeros((NG * 8, 64), F32)
    for k in range(4):
        hit_f = jnp.where(ids_row[k] == expert_f, 1.0, hit_f)
    lane = lax.broadcasted_iota(jnp.int32, (64, 64), 1)
    sub = lax.broadcasted_iota(jnp.int32, (64, 64), 0)
    upper = jnp.where((sub < lane) & (sub // 32 == lane // 32), 1.0, 0.0).astype(BF)
    lower = jnp.where((lane < sub) & (sub // 32 == lane // 32), 1.0, 0.0).astype(BF)
    earlier = jnp.dot(hit_f.astype(BF), upper, preferred_element_type=F32)
    side = lax.broadcasted_iota(jnp.int32, (NG * 8, 64), 1) // 32
    pick = jnp.where(
        (earlier == rank.astype(F32)) & (side == part), hit_f, 0.0
    ).astype(BF)

    slot_l = lax.broadcasted_iota(jnp.int32, (1, NG * 8), 1)
    expert_l, part_l, rank_l = experts_of(slot_l)
    expert_lf = expert_l.astype(F32)
    hit_lf = jnp.zeros((64, NG * 8), F32)
    for k in range(4):
        hit_lf = jnp.where(ids_col[k] == expert_lf, 1.0, hit_lf)
    earlier_l = jnp.dot(lower, hit_lf.astype(BF), preferred_element_type=F32)
    side_l = lax.broadcasted_iota(jnp.int32, (64, NG * 8), 0) // 32
    pick_l = jnp.where(
        (earlier_l == rank_l.astype(F32)) & (side_l == part_l), hit_lf, 0.0
    )
    to_slot = jnp.where(
        lax.broadcasted_iota(jnp.int32, (64, NG * 8), 0) == expert_l, 1.0, 0.0
    ).astype(BF)

    loads[0].wait()
    loads[1].wait()
    heads_out = attend(q_ref, k_new, v_new, keys, values, lens, starts, qs, hs)
    loads[2].wait()

    def realign(raw, out, load):
        load.wait()
        out[:, :, QW:] = jnp.zeros((ND, 360, PW - QW), BF)

        def shift_rows(i, carry):
            rows = pl.ds(pl.multiple_of(i * 16, 16), 16)
            for q in range(4):
                out[q, rows, 0:QW] = raw[rows, QW * q : QW * (q + 1)]
            return carry

        lax.fori_loop(0, 22, shift_rows, 0)
        for q in range(4):
            out[q, 352:360, 0:QW] = raw[352:360, QW * q : QW * (q + 1)]

    sums = []
    for i, block in enumerate((opp_q, left_q, right_q, me_q)):
        rows = pl.ds(pl.multiple_of(block * QW, 16), QW)
        part_sum = lax.dot_general(
            heads_out, wo[rows, :], (((1,), (1,)), ((), ())), preferred_element_type=F32
        )
        proj[i, :, 0:QW] = part_sum.astype(BF)
    pl.semaphore_wait(barrier, NG - 1 + 3)
    for i in range(3):
        copy = pltpu.make_async_remote_copy(
            src_ref=proj.at[i], dst_ref=rs.at[i], send_sem=rs_ss.at[i],
            recv_sem=rs_rs.at[i], device_id=peers[i], device_id_type=MESH,
        )
        copy.start()
        sums.append(copy)
    attended = proj[3, :, 0:QW].astype(F32) + resid[...].astype(F32)
    for i in (1, 2, 0):
        sums[i].wait_recv()
        attended = attended + rs[i, :, 0:QW].astype(F32)
    attended = jnp.concatenate([attended, jnp.zeros((32, PW - QW), F32)], axis=1)
    att = attended.astype(BF)
    halves = jnp.concatenate([att[:, :HW], att[:, HW:]], axis=0)
    send[...] = (
        jnp.dot(pick, halves, preferred_element_type=F32).reshape(NG, 8, HW).astype(BF)
    )
    own_msg = pltpu.make_async_copy(send.at[0], recv.at[0, 0], a_rs.at[0])
    own_msg.start()

    def post(j):
        def post_one(k, carry):
            pltpu.make_async_remote_copy(
                src_ref=send.at[k], dst_ref=recv.at[0, k], send_sem=a_ss.at[j],
                recv_sem=a_rs.at[j], device_id={"grp": grp_shift(z, y, c, k, 1)},
                device_id_type=MESH,
            ).start()
            return carry

        lax.fori_loop(max(1, j * JM), (j + 1) * JM, post_one, 0)

    def posted(j):
        first = max(1, j * JM)
        wait_bytes(send.at[pl.ds(first, (j + 1) * JM - first)], a_ss.at[j])

    for j in range(NJ):
        post(j)
    att_out[...] = att[:, :QW]
    weighted = (attended * gain[pl.ds(me_q, 1), :]).astype(BF)
    stats[...] = jnp.zeros(stats.shape, F32)
    stats[:, 0:64] = lax.dot_general(
        weighted[:, :QW], router[...], (((1,), (1,)), ((), ())), preferred_element_type=F32
    )
    stats[:, 64:65] = jnp.sum(attended * attended, axis=1, keepdims=True)

    shared = [
        pltpu.make_async_remote_copy(
            src_ref=stats, dst_ref=stats_in.at[i], send_sem=st_ss.at[i],
            recv_sem=st_rs.at[i], device_id=peer, device_id_type=MESH,
        )
        for i, peer in enumerate(peers)
    ]
    for copy in shared:
        copy.start()

    realign(wg, wga, loads[3])
    realign(wu, wua, loads[4])
    realign(wd, wda, loads[5])

    first4 = lax.broadcasted_iota(jnp.int32, (BM // 2, 8, HW), 1) < 4

    def to_side(src, dst, ss, rs_, peer):
        return pltpu.make_async_remote_copy(
            src_ref=src, dst_ref=dst, send_sem=ss, recv_sem=rs_, device_id=peer,
            device_id_type=MESH,
        )

    def span(b):
        return pl.ds(b * BM, BM)

    def ring_out(j):
        at = pl.ds(j * JM, JM)
        wait_bytes(recv.at[0, at], a_rs.at[j])
        copies = (
            to_side(recv.at[0, at], recv.at[1, at], x_ss.at[j, 0], x_rs.at[j, 0], right),
            to_side(recv.at[0, at], recv.at[2, at], x_ss.at[j, 1], x_rs.at[j, 1], left),
        )
        for copy in copies:
            copy.start()
        return copies

    def ring_on(j, copies):
        first, second = pl.ds(j * JM, JM // 2), pl.ds(j * JM + JM // 2, JM // 2)
        copies[0].wait_recv()
        on_right = to_side(
            recv.at[1, first], recv.at[3, first], f_ss.at[j, 0], f_rs.at[j, 0], right
        )
        on_right.start()
        copies[1].wait_recv()
        on_left = to_side(
            recv.at[2, second], recv.at[3, second], f_ss.at[j, 1], f_rs.at[j, 1], left
        )
        on_left.start()
        return on_right, on_left

    def expert_out(b, forwards):
        for copy in forwards:
            copy.wait_recv()
        gate = jnp.zeros((BR, 360), F32)
        up = jnp.zeros((BR, 360), F32)
        square = jnp.zeros((BR, 1), F32)
        for i, q in enumerate(blocks):
            rows = recv[i, span(b)].astype(F32).reshape(BM // 2, 2, 8, HW)
            even, odd = rows[:, 0], rows[:, 1]
            low = jnp.where(first4, even, pltpu.roll(odd, 4, 1)).reshape(BR, HW)
            high = jnp.where(first4, pltpu.roll(even, 4, 1), odd).reshape(BR, HW)
            feats = jnp.concatenate([low, high], axis=1)
            square = square + jnp.sum(feats * feats, axis=1, keepdims=True)
            feats = (feats * gain[pl.ds(q, 1), :]).astype(BF)
            last = (((1,), (1,)), ((), ()))
            gate = gate + lax.dot_general(feats, wga[q], last, preferred_element_type=F32)
            up = up + lax.dot_general(feats, wua[q], last, preferred_element_type=F32)
        rms = lax.rsqrt(square / (ND * QW) + EPS)
        gate = gate * rms
        up = up * rms
        act = (gate * jax.nn.sigmoid(1.702 * gate) * (up + 1.0)).astype(BF)
        out = jnp.dot(act, wda[opp_q], preferred_element_type=F32).astype(BF)
        s1s[b, 0] = out[: BR // 2]
        s1s[b, 1] = out[BR // 2 :]
        copies = (
            to_side(s1s.at[b, 0], s1r.at[b, 0], p_ss.at[b, 0], p_rs.at[b, 0], right),
            to_side(s1s.at[b, 1], s1r.at[b, 1], p_ss.at[b, 1], p_rs.at[b, 1], left),
        )
        for copy in copies:
            copy.start()
        for i, q in enumerate((me_q, right_q, left_q)):
            out = jnp.dot(act, wda[q], preferred_element_type=F32)
            own[b, i] = out.astype(BF).astype(F32)
        return copies

    def sum_on(b, firsts):
        firsts[0].wait_recv()
        to_right = own[b, 1]
        s2s[b, 0, 0 : BR // 2] = (to_right[: BR // 2] + s1r[b, 0].astype(F32)).astype(BF)
        s2s[b, 0, BR // 2 :] = to_right[BR // 2 :].astype(BF)
        firsts[1].wait_recv()
        to_left = own[b, 2]
        s2s[b, 1, 0 : BR // 2] = to_left[: BR // 2].astype(BF)
        s2s[b, 1, BR // 2 :] = (to_left[BR // 2 :] + s1r[b, 1].astype(F32)).astype(BF)
        copies = (
            to_side(s2s.at[b, 0], s2r.at[b, 0], q_ss.at[b, 0], q_rs.at[b, 0], right),
            to_side(s2s.at[b, 1], s2r.at[b, 1], q_ss.at[b, 1], q_rs.at[b, 1], left),
        )
        for copy in copies:
            copy.start()
        return copies

    def give_back(b, seconds):
        for copy in seconds:
            copy.wait_recv()
        rows = own[b, 0] + s2r[b, 0].astype(F32) + s2r[b, 1].astype(F32)
        low = rows[:, :HW].reshape(BM // 2, 8, HW)
        high = rows[:, HW:].reshape(BM // 2, 8, HW)
        even = jnp.where(first4, low, pltpu.roll(high, 4, 1))
        odd = jnp.where(first4, pltpu.roll(low, 4, 1), high)
        rsend[b * BM : (b + 1) * BM] = (
            jnp.stack([even, odd], axis=1).reshape(BM, 8, HW).astype(BF)
        )
        if b == 0:
            pltpu.make_async_copy(rsend.at[0], rrecv.at[0], b_rs.at[0]).start()

        def post_back(k, carry):
            pltpu.make_async_remote_copy(
                src_ref=rsend.at[k], dst_ref=rrecv.at[k], send_sem=b_ss, recv_sem=b_rs.at[b],
                device_id={"grp": grp_shift(z, y, c, k, -1)}, device_id_type=MESH,
            ).start()
            return carry

        lax.fori_loop(max(1, b * BM), (b + 1) * BM, post_back, 0)

    out_c = [None] * NJ
    on_c = [None] * NJ
    one_c = [None] * NB
    two_c = [None] * NB

    def run(order):
        for name, i in order:
            if name == "o":
                out_c[i] = ring_out(i)
            elif name == "f":
                on_c[i] = ring_on(i, out_c[i])
            elif name == "e":
                per = NJ // NB
                forwards = [c for pair in on_c[i * per : (i + 1) * per] for c in pair]
                one_c[i] = expert_out(i, forwards)
            elif name == "s":
                two_c[i] = sum_on(i, one_c[i])
            else:
                give_back(i, two_c[i])

    plan = "o0o1f0o2f1o3e0f2e1f3s0e2s1g0e3s2g1s3g2g3"
    run([(plan[n], int(plan[n + 1])) for n in range(0, len(plan), 2)])

    total = stats[...]
    for i, copy in enumerate(shared):
        copy.wait_recv()
        total = total + stats_in[i]
    scale = lax.rsqrt(total[:, 64:65] / (ND * QW) + EPS)
    logits = total[:, 0:64] * scale
    named = jnp.zeros((32, 64), jnp.bool_)
    experts = lax.broadcasted_iota(jnp.int32, (32, 64), 1).astype(F32)
    for k in range(4):
        named = named | (ids_col[k][0:32] == experts)
    lifted = jnp.where(named, jnp.exp(jnp.where(named, logits, 0.0)), 0.0)
    weight = lifted / jnp.sum(lifted, axis=1, keepdims=True)
    weight = jnp.concatenate([weight, weight], axis=0)
    w_high = weight.astype(BF)
    w_low = (weight - w_high.astype(F32)).astype(BF)
    mix_high = (jnp.dot(w_high, to_slot, preferred_element_type=F32) * pick_l).astype(BF)
    mix_low = (jnp.dot(w_low, to_slot, preferred_element_type=F32) * pick_l).astype(BF)

    mixed = jnp.zeros((64, HW), F32)
    for b in range(NB):
        wait_bytes(rrecv.at[span(b)], b_rs.at[b])
        rows = rrecv[b * BM : (b + 1) * BM].reshape(BM * 8, HW)
        cols = slice(b * BM * 8, (b + 1) * BM * 8)
        mixed = mixed + jnp.dot(mix_high[:, cols], rows, preferred_element_type=F32)
        mixed = mixed + jnp.dot(mix_low[:, cols], rows, preferred_element_type=F32)
    mixed = mixed.astype(BF)
    mix_out[:, 0:HW] = mixed[0:32]
    mix_out[:, HW:QW] = mixed[32:64, 0 : QW - HW]

    for copy in sums + shared:
        copy.wait_send()
    for j in range(NJ):
        posted(j)
    wait_bytes(rsend.at[pl.ds(1, NG - 1)], b_ss)
    for group in (out_c, on_c, one_c, two_c):
        for pair in group:
            for copy in pair:
                copy.wait_send()


def hand_on(att, mix, att_out, mix_out):
    att_out[...] = att[...]
    mix_out[...] = mix[...]


def local(
    q_new, k_new, v_new, k_cache, v_cache, cache_len, cycle_start, residual, out_proj,
    norm_gain, router, route_ids, w_gate, w_up, w_down,
):
    vmem = pl.BlockSpec(memory_space=pltpu.VMEM)
    hbm = pl.BlockSpec(memory_space=pl.ANY)
    dma = pltpu.SemaphoreType.DMA
    ff = w_gate.shape[2]
    tokens, heads = q_new.shape
    wide = pltpu.VMEM((ff, ND * QW), BF)
    att, mix = pl.pallas_call(
        stage,
        out_shape=(
            jax.ShapeDtypeStruct(residual.shape, BF),
            jax.ShapeDtypeStruct(residual.shape, BF),
        ),
        in_specs=[vmem] * 3 + [hbm] * 2 + [vmem] * 3 + [hbm] + [vmem] * 3 + [hbm] * 3,
        out_specs=(vmem, vmem),
        scratch_shapes=[
            pltpu.VMEM(k_cache.shape, BF),
            pltpu.VMEM(v_cache.shape, BF),
            pltpu.VMEM((tokens, heads // 128, 128), F32),
            pltpu.VMEM((tokens, heads // 128, 128), F32),
            pltpu.VMEM((ND * QW, heads), BF),
            pltpu.VMEM((ND, tokens, PW), BF),
            pltpu.VMEM((ND, PW), F32),
            wide,
            wide,
            wide,
            pltpu.VMEM((ND, ff, PW), BF),
            pltpu.VMEM((ND, ff, PW), BF),
            pltpu.VMEM((ND, ff, PW), BF),
            pltpu.VMEM((3, 32, PW), BF),
            pltpu.VMEM((32, 128), F32),
            pltpu.VMEM((3, 32, 128), F32),
            pltpu.VMEM((NG, 8, HW), BF),
            pltpu.VMEM((ND, NG, 8, HW), BF),
            pltpu.VMEM((NB, 2, BR // 2, PW), BF),
            pltpu.VMEM((NB, 2, BR // 2, PW), BF),
            pltpu.VMEM((NB, 2, BR, PW), BF),
            pltpu.VMEM((NB, 2, BR, PW), BF),
            pltpu.VMEM((NB, 3, BR, PW), F32),
            pltpu.VMEM((NG, 8, HW), BF),
            pltpu.VMEM((NG, 8, HW), BF),
            dma((6,)),
            dma((3,)),
            dma((3,)),
            dma((3,)),
            dma((3,)),
            dma((NJ,)),
            dma((NJ,)),
            dma((NJ, 2)),
            dma((NJ, 2)),
            dma((NJ, 2)),
            dma((NJ, 2)),
            dma((NB, 2)),
            dma((NB, 2)),
            dma((NB, 2)),
            dma((NB, 2)),
            dma,
            dma((NB,)),
        ],
        compiler_params=pltpu.CompilerParams(collective_id=0, has_side_effects=True),
        name="experts",
    )(
        q_new, k_new, v_new, k_cache, v_cache, cache_len[None], cycle_start[None], residual,
        out_proj.T, norm_gain, router.T, route_ids.T, w_gate[0].T, w_up[0].T, w_down[0],
    )
    return pl.pallas_call(
        hand_on,
        out_shape=(
            jax.ShapeDtypeStruct(residual.shape, BF),
            jax.ShapeDtypeStruct(residual.shape, BF),
        ),
        in_specs=[vmem, vmem],
        out_specs=(vmem, vmem),
        name="hand_on",
    )(att, mix)


def solution(mesh):
    placed = (
        P("grp", ("role", "tp")),
        P("grp", ("role", "tp")),
        P("grp", ("role", "tp")),
        P("grp", None, ("role", "tp")),
        P("grp", None, ("role", "tp")),
        P("grp"),
        P("grp"),
        P("grp", ("role", "tp")),
        P(("role", "tp"), None),
        P(),
        P(("role", "tp"), None),
        P("grp", None),
        P("grp", None, ("role", "tp")),
        P("grp", None, ("role", "tp")),
        P("grp", ("role", "tp"), None),
    )
    return jax.shard_map(
        local,
        mesh=mesh,
        in_specs=placed,
        out_specs=(P("grp", ("role", "tp")), P("grp", ("role", "tp"))),
        check_vma=False,
    )
```

```python
import jax
import jax.numpy as jnp
from jax import lax
from jax.experimental import pallas as pl
from jax.experimental.pallas import tpu as pltpu
from jax.sharding import PartitionSpec as P

HD = 64
EPS = 1e-05
ND = 4
QW = 720
PW = 768
HW = PW // 2
NG = 64
NJ = 4
JM = NG // NJ
NB = 4
BM = NG // NB
BR = BM * 4
MESH = pl.DeviceIdType.MESH
BF = jnp.bfloat16
F32 = jnp.float32


def attend(q_ref, k_new, v_new, keys, values, lens, starts, qs, hs):
    tokens, window = keys.shape[0], keys.shape[1]
    sub = lax.broadcasted_iota(jnp.int32, (tokens, tokens), 0)
    lane = lax.broadcasted_iota(jnp.int32, (tokens, tokens), 1)

    def column(row):
        return jnp.sum(jnp.where(sub == lane, row.astype(F32), 0.0), axis=1, keepdims=True)

    slot = lax.broadcasted_iota(jnp.int32, (tokens, window), 1).astype(F32)
    age = slot - column(starts[...])
    age = jnp.where(age < 0.0, age + window, age)
    live_all = jnp.where(age < column(lens[...]), 1.0, 0.0)
    queries = q_ref[...].astype(F32) * HD ** (-0.5)
    for j in range(8):
        qs[:, j, :] = queries[:, 128 * j : 128 * (j + 1)]
    step = 8
    shape = (step, 8, 128)
    mine = (lax.broadcasted_iota(jnp.int32, shape, 1) < 4) == (
        lax.broadcasted_iota(jnp.int32, shape, 2) < HD
    )
    key_own = k_new[...].astype(F32)
    value_own = v_new[...].astype(F32)
    for start in range(0, tokens, step):
        rows = slice(start, start + step)
        pair = qs[rows]
        heads = jnp.concatenate(
            [jnp.where(mine, pair, 0.0), jnp.where(mine, pltpu.roll(pair, HD, 2), 0.0)], axis=1
        )
        own = jnp.sum(heads * key_own[rows][:, None, :], axis=2, keepdims=True)
        scores = lax.dot_general(
            heads.astype(BF), keys[rows], (((2,), (2,)), ((0,), (0,))),
            preferred_element_type=F32,
        )
        live = jnp.broadcast_to(live_all[rows][:, None, :], scores.shape) > 0.5
        scores = jnp.where(live, scores, -1e30)
        highest = jnp.maximum(jnp.max(scores, axis=2, keepdims=True), own)
        lifted = jnp.where(live, jnp.exp(scores - highest), 0.0)
        own_lift = jnp.exp(own - highest)
        total = jnp.sum(lifted, axis=2, keepdims=True) + own_lift
        weights = (lifted / total).astype(BF)
        own_weight = (own_lift / total).astype(BF).astype(F32)
        out = lax.dot_general(
            weights, values[rows], (((2,), (1,)), ((0,), (0,))), preferred_element_type=F32
        )
        out = out + own_weight * value_own[rows][:, None, :]
        hs[rows] = jnp.where(mine, out[:, 0:8], 0.0) + pltpu.roll(
            jnp.where(mine, out[:, 8:16], 0.0), HD, 2
        )
    return jnp.concatenate([hs[:, j, :] for j in range(8)], axis=1).astype(BF)


def x_of(pos):
    role = pos % 2
    tp = pos // 2
    return {"role": role, "tp": tp}, role * 2 + tp


def grp_shift(z, y, c, k, sign):
    j = lax.div(k, 8)
    half = lax.div(j + 1, 2)
    odd = lax.rem(j, 2)
    dz = odd * half + (1 - odd) * (8 - half)
    dy = lax.rem(lax.div(k, 2), 4)
    dc = lax.rem(k, 2)
    if sign < 0:
        dz = 8 - dz
        dy = 4 - dy
    return (lax.rem(z + dz, 8) * 4 + lax.rem(y + dy, 4)) * 2 + lax.rem(c + dc, 2)


def wait_bytes(ref, sem):
    pltpu.make_async_copy(ref, ref, sem).wait()


def stage(
    q_ref, k_new, v_new, k_hbm, v_hbm, lens, starts, resid, wo_hbm, gain_row, router, ids,
    wg_hbm, wu_hbm, wd_hbm,
    att_out, mix_out,
    keys, values, qs, hs, wo, proj, gain,
    wg, wu, wd, wga, wua, wda, rs, stats, stats_in, send, recv, s1s, s1r, s2s, s2r, own, rsend,
    rrecv,
    w_sem, rs_ss, rs_rs, st_ss, st_rs, a_ss, a_rs, x_ss, x_rs, f_ss, f_rs,
    p_ss, p_rs, q_ss, q_rs, b_ss, b_rs,
):
    r = lax.axis_index("role")
    g = lax.axis_index("grp")
    t = lax.axis_index("tp")
    x = t * 2 + r
    z = g // 8
    y = (g // 2) % 4
    c = g % 2
    me_q = r * 2 + t
    right, right_q = x_of((x + 1) % 4)
    left, left_q = x_of((x + 3) % 4)
    opp, opp_q = x_of((x + 2) % 4)
    peers = (opp, left, right)
    blocks = (me_q, left_q, right_q, opp_q)

    barrier = pltpu.get_barrier_semaphore()

    def greet(k, carry):
        pl.semaphore_signal(
            barrier, inc=1, device_id={"grp": grp_shift(z, y, c, NG - k, 1)},
            device_id_type=MESH,
        )
        return carry

    lax.fori_loop(1, NG, greet, 0)
    for peer in peers:
        pl.semaphore_signal(barrier, inc=1, device_id=peer, device_id_type=MESH)
    loads = [
        pltpu.make_async_copy(src, dst, w_sem.at[i])
        for i, (src, dst) in enumerate(
            (
                (k_hbm, keys), (v_hbm, values), (wo_hbm, wo), (wg_hbm, wg), (wu_hbm, wu),
                (wd_hbm, wd),
            )
        )
    ]
    for load in loads:
        load.start()
    gain[...] = jnp.zeros(gain.shape, F32)
    for q in range(4):
        gain[q : q + 1, 0:QW] = gain_row[QW * q : QW * (q + 1)].reshape(1, QW)
        proj[q, :, QW:] = jnp.zeros((32, PW - QW), BF)

    def experts_of(rows):
        return grp_shift(z, y, c, lax.div(rows, 8), 1), lax.rem(lax.div(rows, 4), 2), lax.rem(rows, 4)

    slot = lax.broadcasted_iota(jnp.int32, (NG * 8, 1), 0)
    expert, part, rank = experts_of(slot)
    lane = lax.broadcasted_iota(jnp.int32, (64, 32), 1)
    sub = lax.broadcasted_iota(jnp.int32, (64, 32), 0)
    ids_f = ids[...].astype(F32)
    ids_col = [
        jnp.sum(jnp.where(sub % 32 == lane, ids_f[k : k + 1, :], 0.0), axis=1, keepdims=True)
        for k in range(4)
    ]
    lane = lax.broadcasted_iota(jnp.int32, (32, 64), 1)
    sub = lax.broadcasted_iota(jnp.int32, (32, 64), 0)
    ids_row = [
        jnp.sum(jnp.where(lane % 32 == sub, ids_col[k][0:32], 0.0), axis=0, keepdims=True)
        for k in range(4)
    ]
    expert_f = expert.astype(F32)
    hit_f = jnp.zeros((NG * 8, 64), F32)
    for k in range(4):
        hit_f = jnp.where(ids_row[k] == expert_f, 1.0, hit_f)
    lane = lax.broadcasted_iota(jnp.int32, (64, 64), 1)
    sub = lax.broadcasted_iota(jnp.int32, (64, 64), 0)
    upper = jnp.where((sub < lane) & (sub // 32 == lane // 32), 1.0, 0.0).astype(BF)
    lower = jnp.where((lane < sub) & (sub // 32 == lane // 32), 1.0, 0.0).astype(BF)
    earlier = jnp.dot(hit_f.astype(BF), upper, preferred_element_type=F32)
    side = lax.broadcasted_iota(jnp.int32, (NG * 8, 64), 1) // 32
    pick = jnp.where(
        (earlier == rank.astype(F32)) & (side == part), hit_f, 0.0
    ).astype(BF)

    slot_l = lax.broadcasted_iota(jnp.int32, (1, NG * 8), 1)
    expert_l, part_l, rank_l = experts_of(slot_l)
    expert_lf = expert_l.astype(F32)
    hit_lf = jnp.zeros((64, NG * 8), F32)
    for k in range(4):
        hit_lf = jnp.where(ids_col[k] == expert_lf, 1.0, hit_lf)
    earlier_l = jnp.dot(lower, hit_lf.astype(BF), preferred_element_type=F32)
    side_l = lax.broadcasted_iota(jnp.int32, (64, NG * 8), 0) // 32
    pick_l = jnp.where(
        (earlier_l == rank_l.astype(F32)) & (side_l == part_l), hit_lf, 0.0
    )
    to_slot = jnp.where(
        lax.broadcasted_iota(jnp.int32, (64, NG * 8), 0) == expert_l, 1.0, 0.0
    ).astype(BF)

    loads[0].wait()
    loads[1].wait()
    heads_out = attend(q_ref, k_new, v_new, keys, values, lens, starts, qs, hs)
    loads[2].wait()

    def realign(raw, out, load):
        load.wait()
        out[:, :, QW:] = jnp.zeros((ND, 360, PW - QW), BF)

        def shift_rows(i, carry):
            rows = pl.ds(pl.multiple_of(i * 16, 16), 16)
            for q in range(4):
                out[q, rows, 0:QW] = raw[rows, QW * q : QW * (q + 1)]
            return carry

        lax.fori_loop(0, 22, shift_rows, 0)
        for q in range(4):
            out[q, 352:360, 0:QW] = raw[352:360, QW * q : QW * (q + 1)]

    sums = []
    for i, block in enumerate((opp_q, left_q, right_q, me_q)):
        rows = pl.ds(pl.multiple_of(block * QW, 16), QW)
        part_sum = lax.dot_general(
            heads_out, wo[rows, :], (((1,), (1,)), ((), ())), preferred_element_type=F32
        )
        proj[i, :, 0:QW] = part_sum.astype(BF)
    pl.semaphore_wait(barrier, NG - 1 + 3)
    for i in range(3):
        copy = pltpu.make_async_remote_copy(
            src_ref=proj.at[i], dst_ref=rs.at[i], send_sem=rs_ss.at[i],
            recv_sem=rs_rs.at[i], device_id=peers[i], device_id_type=MESH,
        )
        copy.start()
        sums.append(copy)
    attended = proj[3, :, 0:QW].astype(F32) + resid[...].astype(F32)
    for i in (1, 2, 0):
        sums[i].wait_recv()
        attended = attended + rs[i, :, 0:QW].astype(F32)
    attended = jnp.concatenate([attended, jnp.zeros((32, PW - QW), F32)], axis=1)
    att = attended.astype(BF)
    halves = jnp.concatenate([att[:, :HW], att[:, HW:]], axis=0)
    send[...] = (
        jnp.dot(pick, halves, preferred_element_type=F32).reshape(NG, 8, HW).astype(BF)
    )
    own_msg = pltpu.make_async_copy(send.at[0], recv.at[0, 0], a_rs.at[0])
    own_msg.start()

    def post(j):
        def post_one(k, carry):
            pltpu.make_async_remote_copy(
                src_ref=send.at[k], dst_ref=recv.at[0, k], send_sem=a_ss.at[j],
                recv_sem=a_rs.at[j], device_id={"grp": grp_shift(z, y, c, k, 1)},
                device_id_type=MESH,
            ).start()
            return carry

        lax.fori_loop(max(1, j * JM), (j + 1) * JM, post_one, 0)

    def posted(j):
        first = max(1, j * JM)
        wait_bytes(send.at[pl.ds(first, (j + 1) * JM - first)], a_ss.at[j])

    for j in range(NJ):
        post(j)
    att_out[...] = att[:, :QW]
    weighted = (attended * gain[pl.ds(me_q, 1), :]).astype(BF)
    stats[...] = jnp.zeros(stats.shape, F32)
    stats[:, 0:64] = lax.dot_general(
        weighted[:, :QW], router[...], (((1,), (1,)), ((), ())), preferred_element_type=F32
    )
    stats[:, 64:65] = jnp.sum(attended * attended, axis=1, keepdims=True)

    shared = [
        pltpu.make_async_remote_copy(
            src_ref=stats, dst_ref=stats_in.at[i], send_sem=st_ss.at[i],
            recv_sem=st_rs.at[i], device_id=peer, device_id_type=MESH,
        )
        for i, peer in enumerate(peers)
    ]
    for copy in shared:
        copy.start()

    realign(wg, wga, loads[3])
    realign(wu, wua, loads[4])
    realign(wd, wda, loads[5])

    first4 = lax.broadcasted_iota(jnp.int32, (BM // 2, 8, HW), 1) < 4

    def to_side(src, dst, ss, rs_, peer):
        return pltpu.make_async_remote_copy(
            src_ref=src, dst_ref=dst, send_sem=ss, recv_sem=rs_, device_id=peer,
            device_id_type=MESH,
        )

    def span(b):
        return pl.ds(b * BM, BM)

    def ring_out(j):
        at = pl.ds(j * JM, JM)
        wait_bytes(recv.at[0, at], a_rs.at[j])
        copies = (
            to_side(recv.at[0, at], recv.at[1, at], x_ss.at[j, 0], x_rs.at[j, 0], right),
            to_side(recv.at[0, at], recv.at[2, at], x_ss.at[j, 1], x_rs.at[j, 1], left),
        )
        for copy in copies:
            copy.start()
        return copies

    def ring_on(j, copies):
        first, second = pl.ds(j * JM, JM // 2), pl.ds(j * JM + JM // 2, JM // 2)
        copies[0].wait_recv()
        on_right = to_side(
            recv.at[1, first], recv.at[3, first], f_ss.at[j, 0], f_rs.at[j, 0], right
        )
        on_right.start()
        copies[1].wait_recv()
        on_left = to_side(
            recv.at[2, second], recv.at[3, second], f_ss.at[j, 1], f_rs.at[j, 1], left
        )
        on_left.start()
        return on_right, on_left

    def expert_out(b, forwards):
        for copy in forwards:
            copy.wait_recv()
        gate = jnp.zeros((BR, 360), F32)
        up = jnp.zeros((BR, 360), F32)
        square = jnp.zeros((BR, 1), F32)
        for i, q in enumerate(blocks):
            rows = recv[i, span(b)].astype(F32).reshape(BM // 2, 2, 8, HW)
            even, odd = rows[:, 0], rows[:, 1]
            low = jnp.where(first4, even, pltpu.roll(odd, 4, 1)).reshape(BR, HW)
            high = jnp.where(first4, pltpu.roll(even, 4, 1), odd).reshape(BR, HW)
            feats = jnp.concatenate([low, high], axis=1)
            square = square + jnp.sum(feats * feats, axis=1, keepdims=True)
            feats = (feats * gain[pl.ds(q, 1), :]).astype(BF)
            last = (((1,), (1,)), ((), ()))
            gate = gate + lax.dot_general(feats, wga[q], last, preferred_element_type=F32)
            up = up + lax.dot_general(feats, wua[q], last, preferred_element_type=F32)
        rms = lax.rsqrt(square / (ND * QW) + EPS)
        gate = gate * rms
        up = up * rms
        act = (gate * jax.nn.sigmoid(1.702 * gate) * (up + 1.0)).astype(BF)
        out = jnp.dot(act, wda[opp_q], preferred_element_type=F32).astype(BF)
        s1s[b, 0] = out[: BR // 2]
        s1s[b, 1] = out[BR // 2 :]
        copies = (
            to_side(s1s.at[b, 0], s1r.at[b, 0], p_ss.at[b, 0], p_rs.at[b, 0], right),
            to_side(s1s.at[b, 1], s1r.at[b, 1], p_ss.at[b, 1], p_rs.at[b, 1], left),
        )
        for copy in copies:
            copy.start()
        for i, q in enumerate((me_q, right_q, left_q)):
            out = jnp.dot(act, wda[q], preferred_element_type=F32)
            own[b, i] = out.astype(BF).astype(F32)
        return copies

    def sum_on(b, firsts):
        firsts[0].wait_recv()
        to_right = own[b, 1]
        s2s[b, 0, 0 : BR // 2] = (to_right[: BR // 2] + s1r[b, 0].astype(F32)).astype(BF)
        s2s[b, 0, BR // 2 :] = to_right[BR // 2 :].astype(BF)
        firsts[1].wait_recv()
        to_left = own[b, 2]
        s2s[b, 1, 0 : BR // 2] = to_left[: BR // 2].astype(BF)
        s2s[b, 1, BR // 2 :] = (to_left[BR // 2 :] + s1r[b, 1].astype(F32)).astype(BF)
        copies = (
            to_side(s2s.at[b, 0], s2r.at[b, 0], q_ss.at[b, 0], q_rs.at[b, 0], right),
            to_side(s2s.at[b, 1], s2r.at[b, 1], q_ss.at[b, 1], q_rs.at[b, 1], left),
        )
        for copy in copies:
            copy.start()
        return copies

    def give_back(b, seconds):
        for copy in seconds:
            copy.wait_recv()
        rows = own[b, 0] + s2r[b, 0].astype(F32) + s2r[b, 1].astype(F32)
        low = rows[:, :HW].reshape(BM // 2, 8, HW)
        high = rows[:, HW:].reshape(BM // 2, 8, HW)
        even = jnp.where(first4, low, pltpu.roll(high, 4, 1))
        odd = jnp.where(first4, pltpu.roll(low, 4, 1), high)
        rsend[b * BM : (b + 1) * BM] = (
            jnp.stack([even, odd], axis=1).reshape(BM, 8, HW).astype(BF)
        )
        if b == 0:
            pltpu.make_async_copy(rsend.at[0], rrecv.at[0], b_rs.at[0]).start()

        def post_back(k, carry):
            pltpu.make_async_remote_copy(
                src_ref=rsend.at[k], dst_ref=rrecv.at[k], send_sem=b_ss, recv_sem=b_rs.at[b],
                device_id={"grp": grp_shift(z, y, c, k, -1)}, device_id_type=MESH,
            ).start()
            return carry

        lax.fori_loop(max(1, b * BM), (b + 1) * BM, post_back, 0)

    out_c = [None] * NJ
    on_c = [None] * NJ
    one_c = [None] * NB
    two_c = [None] * NB

    def run(order):
        for name, i in order:
            if name == "o":
                out_c[i] = ring_out(i)
            elif name == "f":
                on_c[i] = ring_on(i, out_c[i])
            elif name == "e":
                per = NJ // NB
                forwards = [c for pair in on_c[i * per : (i + 1) * per] for c in pair]
                one_c[i] = expert_out(i, forwards)
            elif name == "s":
                two_c[i] = sum_on(i, one_c[i])
            else:
                give_back(i, two_c[i])

    plan = "o1o3f1o2f3o0e1f2e3f0s1e2s3g1e0s2g3s0g2g0"
    run([(plan[n], int(plan[n + 1])) for n in range(0, len(plan), 2)])

    total = stats[...]
    for i, copy in enumerate(shared):
        copy.wait_recv()
        total = total + stats_in[i]
    scale = lax.rsqrt(total[:, 64:65] / (ND * QW) + EPS)
    logits = total[:, 0:64] * scale
    named = jnp.zeros((32, 64), jnp.bool_)
    experts = lax.broadcasted_iota(jnp.int32, (32, 64), 1).astype(F32)
    for k in range(4):
        named = named | (ids_col[k][0:32] == experts)
    lifted = jnp.where(named, jnp.exp(jnp.where(named, logits, 0.0)), 0.0)
    weight = lifted / jnp.sum(lifted, axis=1, keepdims=True)
    weight = jnp.concatenate([weight, weight], axis=0)
    w_high = weight.astype(BF)
    w_low = (weight - w_high.astype(F32)).astype(BF)
    mix_high = (jnp.dot(w_high, to_slot, preferred_element_type=F32) * pick_l).astype(BF)
    mix_low = (jnp.dot(w_low, to_slot, preferred_element_type=F32) * pick_l).astype(BF)

    mixed = jnp.zeros((64, HW), F32)
    for b in range(NB):
        wait_bytes(rrecv.at[span(b)], b_rs.at[b])
        rows = rrecv[b * BM : (b + 1) * BM].reshape(BM * 8, HW)
        cols = slice(b * BM * 8, (b + 1) * BM * 8)
        mixed = mixed + jnp.dot(mix_high[:, cols], rows, preferred_element_type=F32)
        mixed = mixed + jnp.dot(mix_low[:, cols], rows, preferred_element_type=F32)
    mixed = mixed.astype(BF)
    mix_out[:, 0:HW] = mixed[0:32]
    mix_out[:, HW:QW] = mixed[32:64, 0 : QW - HW]

    for copy in sums + shared:
        copy.wait_send()
    for j in range(NJ):
        posted(j)
    wait_bytes(rsend.at[pl.ds(1, NG - 1)], b_ss)
    for group in (out_c, on_c, one_c, two_c):
        for pair in group:
            for copy in pair:
                copy.wait_send()


def hand_on(att, mix, att_out, mix_out):
    att_out[...] = att[...]
    mix_out[...] = mix[...]


def local(
    q_new, k_new, v_new, k_cache, v_cache, cache_len, cycle_start, residual, out_proj,
    norm_gain, router, route_ids, w_gate, w_up, w_down,
):
    vmem = pl.BlockSpec(memory_space=pltpu.VMEM)
    hbm = pl.BlockSpec(memory_space=pl.ANY)
    dma = pltpu.SemaphoreType.DMA
    ff = w_gate.shape[2]
    tokens, heads = q_new.shape
    wide = pltpu.VMEM((ff, ND * QW), BF)
    att, mix = pl.pallas_call(
        stage,
        out_shape=(
            jax.ShapeDtypeStruct(residual.shape, BF),
            jax.ShapeDtypeStruct(residual.shape, BF),
        ),
        in_specs=[vmem] * 3 + [hbm] * 2 + [vmem] * 3 + [hbm] + [vmem] * 3 + [hbm] * 3,
        out_specs=(vmem, vmem),
        scratch_shapes=[
            pltpu.VMEM(k_cache.shape, BF),
            pltpu.VMEM(v_cache.shape, BF),
            pltpu.VMEM((tokens, heads // 128, 128), F32),
            pltpu.VMEM((tokens, heads // 128, 128), F32),
            pltpu.VMEM((ND * QW, heads), BF),
            pltpu.VMEM((ND, tokens, PW), BF),
            pltpu.VMEM((ND, PW), F32),
            wide,
            wide,
            wide,
            pltpu.VMEM((ND, ff, PW), BF),
            pltpu.VMEM((ND, ff, PW), BF),
            pltpu.VMEM((ND, ff, PW), BF),
            pltpu.VMEM((3, 32, PW), BF),
            pltpu.VMEM((32, 128), F32),
            pltpu.VMEM((3, 32, 128), F32),
            pltpu.VMEM((NG, 8, HW), BF),
            pltpu.VMEM((ND, NG, 8, HW), BF),
            pltpu.VMEM((NB, 2, BR // 2, PW), BF),
            pltpu.VMEM((NB, 2, BR // 2, PW), BF),
            pltpu.VMEM((NB, 2, BR, PW), BF),
            pltpu.VMEM((NB, 2, BR, PW), BF),
            pltpu.VMEM((NB, 3, BR, PW), F32),
            pltpu.VMEM((NG, 8, HW), BF),
            pltpu.VMEM((NG, 8, HW), BF),
            dma((6,)),
            dma((3,)),
            dma((3,)),
            dma((3,)),
            dma((3,)),
            dma((NJ,)),
            dma((NJ,)),
            dma((NJ, 2)),
            dma((NJ, 2)),
            dma((NJ, 2)),
            dma((NJ, 2)),
            dma((NB, 2)),
            dma((NB, 2)),
            dma((NB, 2)),
            dma((NB, 2)),
            dma,
            dma((NB,)),
        ],
        compiler_params=pltpu.CompilerParams(collective_id=0, has_side_effects=True),
        name="experts",
    )(
        q_new, k_new, v_new, k_cache, v_cache, cache_len[None], cycle_start[None], residual,
        out_proj.T, norm_gain, router.T, route_ids.T, w_gate[0].T, w_up[0].T, w_down[0],
    )
    return pl.pallas_call(
        hand_on,
        out_shape=(
            jax.ShapeDtypeStruct(residual.shape, BF),
            jax.ShapeDtypeStruct(residual.shape, BF),
        ),
        in_specs=[vmem, vmem],
        out_specs=(vmem, vmem),
        name="hand_on",
    )(att, mix)


def solution(mesh):
    placed = (
        P("grp", ("role", "tp")),
        P("grp", ("role", "tp")),
        P("grp", ("role", "tp")),
        P("grp", None, ("role", "tp")),
        P("grp", None, ("role", "tp")),
        P("grp"),
        P("grp"),
        P("grp", ("role", "tp")),
        P(("role", "tp"), None),
        P(),
        P(("role", "tp"), None),
        P("grp", None),
        P("grp", None, ("role", "tp")),
        P("grp", None, ("role", "tp")),
        P("grp", ("role", "tp"), None),
    )
    return jax.shard_map(
        local,
        mesh=mesh,
        in_specs=placed,
        out_specs=(P("grp", ("role", "tp")), P("grp", ("role", "tp"))),
        check_vma=False,
    )
```
